512 devices in a mesh: sky: 64 (over z, y_hi, core), ccd: 8 (over x, y_lo).
Axes of the slice: x: 4, y: 8 (y_hi: 4, y_lo: 2; y = y_hi * 2 + y_lo), z: 8, core: 2. Of those that a mesh axis runs over, the one named last changes fastest.
Arguments:
- science: bfloat16 [384, 1024, 256], P('sky', 'ccd'), may hold values from -6 to 6
- templates: bfloat16 [1024, 1024, 128], P('sky', 'ccd'), may hold values from -6 to 6
- cell_owner: int32 [64, 288, 1], P('sky', 'ccd'), may hold values from 0 to 63; in each aligned block of 36 rows (0 to 35, 36 to 71, ..., all dimensions but the last counted through in order) at most 2 rows name the same one
- cell_index: int32 [64, 288], P('sky', 'ccd'), may hold values from 0 to 15
- row_offset: int32 [384, 8], P('sky', 'ccd'), may hold values from 0 to 98
- col_offset: int32 [384, 8], P('sky', 'ccd'), may hold values from 0 to 98
- coefficients: float32 [384, 8, 21, 6], P('sky', 'ccd'), may hold values from -1.8 to 1.8
- psf_taps: bfloat16 [384, 2, 31], P('sky'), may hold values from 0.029907227 to 0.29882812
Outputs:
- difference: bfloat16 [384, 1024, 256], P('sky', 'ccd')
- score: float32 [384, 1024, 256], P('sky', 'ccd')
The draws below stay inside these ranges and needn't reach their ends.
Inputs may be any that keep to these rules, and one draw needn't show every extreme that they name: `cell_owner`: within the rows of one device, no owner appears more than 2 times.
All inputs are finite; a program needn't handle non-finite values.
Results may differ from the reference program's by a relative error of at most 0.0062.
Values may be sent and summed in bfloat16 or wider, within the bound.
No kernel may reach another device: no remote copies, remote signals or barrier semaphores. Data moves between devices by JAX's collectives and lax.ppermute only.
A program may use at most 128 MiB of HBM per device.

```python
import math
import jax
import jax.numpy as jnp
import numpy as np
from jax import lax

TILE_ROWS = 128
TILE_COLS = 256
RAD = 15
TAPS = 31
NBASIS = 21
NPOLY = 6
CELL = 128
CELL_DEV = 16
VIS_DEV = 6
VISITS = 384
ROWS = 1024
CROWS = 2
CCOLS = 3
CPV = 6
REQ = 36
CAP = 2
MAXOY = 98
MAXOX = 98
N_SKY = 64
N_CCD = 8


def set_ends(result, stream_key, least, high):
    index_at = [jax.random.randint(jax.random.fold_in(stream_key, axis), (), 0, length) for axis, length in enumerate(result.shape)]
    widest = result.shape.index(max(result.shape))
    beside = index_at[:widest] + [(index_at[widest] + 1) % result.shape[widest]] + index_at[widest + 1:]
    return result.at[tuple(index_at)].set(least).at[tuple(beside)].set(high)


def levels(stream_key, dims, split, least, high):
    gain = 1.0
    for dim, parts in split:
        draws = jax.random.uniform(jax.random.fold_in(jax.random.fold_in(stream_key, 6), dim), (parts,), jnp.float32, least / len(split), high / len(split))
        gain = gain * jnp.repeat(jnp.exp(draws), dims[dim] // parts).reshape((-1,) + (1,) * (len(dims) - 1 - dim))
    return gain


def assign_block(key, own, number, rows, count, top, bound, lean):
    ranking = jax.random.permutation(key, count)
    crowded, ordinary = shares(count, rows * top, bound, lean, True), shares(count, rows * top, bound, lean, False)
    places = jnp.arange(count)

    def named(lengths, rotation):
        used = int((lengths > 0).sum())
        fixed = max(1, used // 4)
        shifted = fixed + (places - fixed + rotation * (used - fixed)) % max(1, count - fixed)
        return jnp.zeros((count,), jnp.int32).at[ranking[jnp.where(places < fixed, places, shifted)]].set(jnp.asarray(lengths, jnp.int32))

    lengths = jnp.where(number % 4 == 0, named(crowded, number // 4), named(ordinary, number - number // 4 - 1))
    mixed = jax.random.permutation(jax.random.fold_in(own, 3), count)
    donor, sink = mixed[0:count // 2 * 2:2], mixed[1:count // 2 * 2:2]
    room = jnp.minimum(lengths[donor] - 1, bound - lengths[sink]) // 2
    room = jnp.where((donor == ranking[0]) | (sink == ranking[0]) | (lengths[sink] == 0), 0, jnp.maximum(room, 0))
    shifted = jax.random.randint(jax.random.fold_in(own, 4), (count // 2,), 0, 1 << 20) % (room + 1)
    lengths = lengths.at[donor].add(-shifted).at[sink].add(shifted)
    members = jnp.searchsorted(jnp.cumsum(lengths), jnp.arange(rows * top), side="right").astype(jnp.int32)
    table = members.reshape(top, rows).T
    table = table[jax.random.permutation(jax.random.fold_in(own, 1), rows)]
    rotation = jax.random.randint(jax.random.fold_in(own, 2), (rows, 1), 0, top)
    return jnp.take_along_axis(table, (jnp.arange(top)[None, :] + rotation) % top, axis=1)


def shares(count, total, reach, lean, full):
    weights = [(1 << 20) // math.isqrt(standing ** lean) + 1 for standing in range(1, count + 1)]
    largest = reach if full else min(reach, max(-(-total // count), total * weights[0] // sum(weights)))
    least = 1 if total - largest >= count - 1 else 0
    counts, spare = [largest] + [least] * (count - 1), total - largest - least * (count - 1)
    while spare > 0:
        free = [i for i in range(1, count) if counts[i] < largest] or [i for i in range(1, count) if counts[i] < reach]
        mass, left = sum([weights[i] for i in free]), spare
        for i in free:
            extra = min(reach - counts[i], max(1, left * weights[i] // mass), spare)
            counts[i] = counts[i] + extra
            spare = spare - extra
    return np.array(counts)


def gaussian(own_key, dims, width, bound, pieces=(), kind=jnp.bfloat16):
    entries = jax.random.normal(own_key, dims, jnp.float32) * width
    if len(pieces) > 0:
        entries = levels(own_key, dims, pieces, -0.22, 0.18) * entries
    return jnp.clip(entries, min=-bound, max=bound).astype(kind)


def setup_inputs(seed: int = 0) -> dict:
    arg_keys = jax.random.split(jax.random.key(seed), 9)
    science = gaussian(arg_keys[0], (VISITS, ROWS, TILE_COLS), 1.0, 6.0, ((0, 64), (1, 8)))
    templates = gaussian(arg_keys[1], (N_SKY * CELL_DEV, N_CCD * CELL, CELL), 1.0, 6.0, ((0, 64), (1, 8)))
    cell_owner_keys = jax.random.split(jax.random.fold_in(arg_keys[2], 1), N_SKY * (N_CCD * REQ) // REQ)
    cell_owner_turns = jax.random.permutation(jax.random.fold_in(arg_keys[2], 3), N_SKY * (N_CCD * REQ) // REQ)
    cell_owner = jax.vmap(lambda own, number: assign_block(jax.random.fold_in(arg_keys[2], 2), own, number, REQ, N_SKY, 1, CAP, 2))(cell_owner_keys, cell_owner_turns).reshape((N_SKY, N_CCD * REQ, 1))
    cell_index = set_ends(jax.random.randint(arg_keys[3], (N_SKY, N_CCD * REQ), 0, CELL_DEV), jax.random.fold_in(arg_keys[3], 1), 0, CELL_DEV - 1).astype(jnp.int32)
    row_offset = set_ends(jax.random.randint(arg_keys[4], (VISITS, N_CCD), 0, MAXOY + 1), jax.random.fold_in(arg_keys[4], 1), 0, MAXOY).astype(jnp.int32)
    col_offset = set_ends(jax.random.randint(arg_keys[5], (VISITS, N_CCD), 0, MAXOX + 1), jax.random.fold_in(arg_keys[5], 1), 0, MAXOX).astype(jnp.int32)
    coefficients = gaussian(arg_keys[6], (VISITS, N_CCD, NBASIS, NPOLY), 0.3, 1.8, ((0, 64), (1, 8)), jnp.float32)
    psf_taps = jnp.clip(jnp.exp(math.log(0.29882812) - 2.30176843 * jax.random.uniform(arg_keys[7], (VISITS, 2, TAPS), jnp.float32) ** levels(arg_keys[7], (VISITS, 2, TAPS), ((0, 64),), -0.2, 0.2)), 0.029907227, 0.29882812).astype(jnp.bfloat16)
    return dict(science=science, templates=templates, cell_owner=cell_owner, cell_index=cell_index, row_offset=row_offset, col_offset=col_offset, coefficients=coefficients, psf_taps=psf_taps)


basis_width = 4.0

def hermite_taps():
    scaled = (jnp.arange(2 * RAD + 1, dtype=jnp.float32) - RAD) / basis_width
    series = [jnp.ones(scaled.shape, jnp.float32), 2.0 * scaled]
    for degree in range(1, 5):
        series.append(2.0 * scaled * series[degree] - 2.0 * degree * series[degree - 1])
    weighted = jnp.stack(series) * jnp.exp(-0.5 * scaled * scaled)
    weighted = weighted / jnp.sqrt(lax.optimization_barrier(jnp.sum(weighted * weighted, axis=1, keepdims=True)))
    return weighted.astype(jnp.bfloat16)

def band_matrix(tap_table, count_in, count_out, tap_shift):
    lag_grid = jnp.arange(count_in, dtype=jnp.int32)[None, :] - jnp.arange(count_out, dtype=jnp.int32)[:, None] + tap_shift
    hit_grid = (lag_grid[:, :, None] == jnp.arange(tap_table.shape[-1], dtype=jnp.int32)[None, None, :]).astype(jnp.float32)
    return jnp.einsum('oiu,ku->koi', hit_grid, tap_table.astype(jnp.float32))

def poly_grid(row_count, col_count):
    row_pos = (2.0 * jnp.arange(row_count, dtype=jnp.float32) + 1.0) / row_count - 1.0
    col_pos = (2.0 * jnp.arange(col_count, dtype=jnp.float32) + 1.0) / col_count - 1.0
    across_pos = jnp.broadcast_to(col_pos[None, :], (row_count, col_count))
    down_pos = jnp.broadcast_to(row_pos[:, None], (row_count, col_count))
    return jnp.stack([jnp.ones_like(across_pos), across_pos, down_pos, across_pos * across_pos, across_pos * down_pos, down_pos * down_pos])

def reference(science, templates, cell_owner, cell_index, row_offset, col_offset, coefficients, psf_taps):
    hermite = hermite_taps()
    across_bands = band_matrix(hermite, TILE_COLS + 2 * RAD, TILE_COLS, 0)
    down_bands = band_matrix(hermite, TILE_ROWS + 2 * RAD, TILE_ROWS, 0)
    poly_terms = poly_grid(TILE_ROWS, TILE_COLS)
    cell_store = templates.reshape(N_SKY, CELL_DEV, N_CCD, CELL, CELL)
    owner_table = cell_owner[:, :, 0].astype(jnp.int32)
    index_table = cell_index.astype(jnp.int32)
    row_table = row_offset.astype(jnp.int32)
    col_table = col_offset.astype(jnp.int32)
    zero_index = jnp.zeros((), jnp.int32)

    def one_tile(tile_id):
        visit_id = (tile_id // N_CCD).astype(jnp.int32)
        chip_id = (tile_id % N_CCD).astype(jnp.int32)
        sky_group = (visit_id // VIS_DEV).astype(jnp.int32)
        first_row = (chip_id * REQ + visit_id % VIS_DEV * CPV).astype(jnp.int32)
        owners = lax.dynamic_slice(owner_table, (sky_group, first_row), (1, CPV))[0]
        picked = lax.dynamic_slice(index_table, (sky_group, first_row), (1, CPV))[0]
        cell_stack = cell_store[owners, picked, chip_id]
        assembled = cell_stack.reshape(CROWS, CCOLS, CELL, CELL).transpose(0, 2, 1, 3).reshape(CROWS * CELL, CCOLS * CELL)
        top_row = row_table[visit_id, chip_id].astype(jnp.int32)
        left_col = col_table[visit_id, chip_id].astype(jnp.int32)
        window = lax.dynamic_slice(assembled, (top_row, left_col), (TILE_ROWS + 2 * RAD, TILE_COLS + 2 * RAD)).astype(jnp.float32)
        across = jnp.einsum('yw,ixw->iyx', window, across_bands).astype(jnp.bfloat16)
        across = lax.optimization_barrier(across).astype(jnp.float32)
        coef_rows = coefficients[visit_id, chip_id]
        model_image = jnp.zeros((TILE_ROWS, TILE_COLS), jnp.float32)
        basis_start = 0
        for hx_order in range(6):
            keep_count = 6 - hx_order
            down_pass = jnp.einsum('jyz,zx->jyx', down_bands[:keep_count], across[hx_order])
            coef_slice = coef_rows[basis_start:basis_start + keep_count]
            coef_maps = lax.optimization_barrier(jnp.sum(coef_slice[:, :, None, None] * poly_terms[None], axis=1))
            model_image = model_image + lax.optimization_barrier(jnp.sum(coef_maps * down_pass, axis=0))
            basis_start = basis_start + keep_count
        tile_start = (chip_id * TILE_ROWS).astype(jnp.int32)
        sci_tile = lax.dynamic_slice(science[visit_id], (tile_start, zero_index), (TILE_ROWS, TILE_COLS)).astype(jnp.float32)
        return (sci_tile - model_image).astype(jnp.bfloat16)
    diff_tiles = lax.map(one_tile, jnp.arange(VISITS * N_CCD, dtype=jnp.int32))
    difference = diff_tiles.reshape(VISITS, ROWS, TILE_COLS)
    psf_values = psf_taps.astype(jnp.float32)

    def filter_visit(visit_id):
        diff_image = difference[visit_id].astype(jnp.float32)
        padded = jnp.pad(diff_image, ((0, 0), (RAD, RAD)))
        across_sum = jnp.zeros((ROWS, TILE_COLS), jnp.float32)
        for tap_pos in range(2 * RAD + 1):
            across_sum = across_sum + psf_values[visit_id, 1, tap_pos] * padded[:, tap_pos:tap_pos + TILE_COLS]
        filtered = lax.optimization_barrier(across_sum.astype(jnp.bfloat16)).astype(jnp.float32)
        padded_rows = jnp.pad(filtered, ((RAD, RAD), (0, 0)))
        score_image = jnp.zeros((ROWS, TILE_COLS), jnp.float32)
        for tap_pos in range(2 * RAD + 1):
            score_image = score_image + psf_values[visit_id, 0, tap_pos] * padded_rows[tap_pos:tap_pos + ROWS]
        return score_image
    score_all = lax.map(filter_visit, jnp.arange(VISITS, dtype=jnp.int32))
    return (difference, score_all)
```

```python
import jax
import jax.numpy as jnp
import numpy as np
from jax import lax
from jax.experimental import pallas as pl
from jax.experimental.pallas import tpu as pltpu
from jax.sharding import PartitionSpec as P

RAD = 15
TAPS = 31
ORDERS = 6
GROUP = 64
CELLS = 16
SIDE = 128
VISITS = 6
COLS = 256
HALO = 16
STRIPE = 32
PACKED = 40
PICKS = 54
PICKPAD = 56
MAXOFF = 98
FAR = 256
f32 = jnp.float32
bf16 = jnp.bfloat16
VM = pl.BlockSpec(memory_space=pltpu.VMEM)
SM = pl.BlockSpec(memory_space=pltpu.SMEM)


def hermite_table():
    t = (np.arange(TAPS, dtype=np.float32) - np.float32(RAD)) / np.float32(4.0)
    series = [np.ones(t.shape, np.float32), np.float32(2.0) * t]
    for n in range(1, ORDERS - 1):
        series.append(np.float32(2.0) * t * series[n] - np.float32(2.0 * n) * series[n - 1])
    w = np.stack(series) * np.exp(np.float32(-0.5) * t * t)
    w = w / np.sqrt(np.sum(w * w, axis=1, keepdims=True))
    return np.asarray(w, dtype=jnp.bfloat16).astype(np.float32)


def request_selector():
    sel = np.zeros((3 * PICKPAD, 128), np.float32)
    for slot in range(3):
        for v in range(VISITS):
            for b in range(3):
                row = slot * 18 + v * 3 + b
                for late in range(2):
                    a = (0, 1, late)[slot]
                    sel[late * PICKPAD + row, v * 6 + a * 3 + b] = CELLS
                    sel[late * PICKPAD + row, 36 + v * 6 + a * 3 + b] = 1
                sel[2 * PICKPAD + row, 72 + v] = 1
    return sel


def pack_kernel(cells_ref, info_ref, out_ref, wide_ref):
    for k in range(CELLS):
        wide_ref[k * SIDE : (k + 1) * SIDE, :] = cells_ref[k].astype(f32)
    info = jnp.broadcast_to(info_ref[...], (PACKED - STRIPE, 128)).astype(f32)

    def step(d, _):
        low = wide_ref[pl.ds(d, CELLS, stride=SIDE), :]
        high = wide_ref[pl.ds(d + GROUP, CELLS, stride=SIDE), :]
        out_ref[d] = jnp.concatenate([low, high, info], axis=0).astype(bf16)
        return 0

    lax.fori_loop(0, GROUP, step, 0, unroll=8)


def select_kernel(me_ref, stripes_ref, sel_ref, out_ref):
    table = jnp.concatenate(
        [
            stripes_ref[:, 0:CELLS, :].reshape(GROUP * CELLS, 128),
            stripes_ref[:, CELLS:STRIPE, :].reshape(GROUP * CELLS, 128),
        ],
        axis=1,
    )
    info = stripes_ref[:, STRIPE, :]
    info = jnp.concatenate([info, jnp.zeros_like(info)], axis=0)
    seen = lax.dot_general(
        sel_ref[...], info, (((1,), (1,)), ((), ())), preferred_element_type=f32
    )
    late = seen[2 * PICKPAD :] > me_ref[0].astype(f32)
    wanted = jnp.where(late, seen[PICKPAD : 2 * PICKPAD], seen[:PICKPAD])
    slot_row = lax.broadcasted_iota(jnp.int32, (PICKPAD, 128), 0)
    half = jnp.where(slot_row < 18, 1.0, jnp.where(slot_row < 36, 0.0, jnp.where(late, 1.0, 0.0)))
    number = lax.broadcasted_iota(jnp.int32, (PICKPAD, GROUP * CELLS), 1).astype(f32)
    batch = 8

    def step(g, carry):
        want, side = carry
        hot = jnp.concatenate(
            [jnp.where(number == want[:, n : n + 1], 1.0, 0.0) for n in range(batch)], axis=0
        ).astype(bf16)
        got = jnp.dot(hot, table, preferred_element_type=f32)
        for n in range(batch):
            rows = got[n * PICKPAD : (n + 1) * PICKPAD]
            pick = jnp.where(side[:, n : n + 1] > 0.5, rows[:, 128:], rows[:, :128])
            out_ref[g * batch + n] = pick.astype(bf16)
        return pltpu.roll(want, 128 - batch, 1), pltpu.roll(side, 128 - batch, 1)

    lax.fori_loop(0, GROUP // batch, step, (wanted, half))


def bands_kernel(
    oy_ref, ox_ref, coef_ref, taps_ref, rev_ref, psf_ref,
    across_ref, down_ref, colf_ref, rowf_ref, tall_ref, toep_ref, shift_ref,
):
    v = pl.program_id(0)

    def spread(row, count):
        return pltpu.roll(jnp.broadcast_to(row, (count, FAR)), 0, 1, stride=1, stride_axis=0)

    @pl.when(v == 0)
    def _():
        for i in range(ORDERS):
            tall_ref[i] = spread(rev_ref[i : i + 1, :], 360)[:, :128]
            toep_ref[i] = spread(taps_ref[i : i + 1, :], SIDE)

    oy = oy_ref[v]
    ox = ox_ref[v]
    for i in range(ORDERS):
        across_ref[0, :, i * 128 : (i + 1) * 128] = tall_ref[i, pl.ds(MAXOFF - ox, FAR), :].astype(
            bf16
        )
        shift_ref[i] = pltpu.roll(toep_ref[i], oy + 192, 1)
    near = lax.broadcasted_iota(jnp.int32, (COLS, COLS), 0) - lax.broadcasted_iota(
        jnp.int32, (COLS, COLS), 1
    )
    colf_ref[0] = jnp.where(
        jnp.abs(near) <= RAD, spread(psf_ref[0, 0:1, :], COLS), 0.0
    ).astype(bf16)
    rowf_ref[0] = spread(psf_ref[0, 1:2, :], SIDE).astype(bf16)

    left = lax.broadcasted_iota(jnp.int32, (16, 128), 1) < 64

    def step(g, _):
        row = lax.broadcasted_iota(jnp.int32, (16, 128), 0) + g * 16
        ty = (2.0 * row.astype(f32) + 1.0) / SIDE - 1.0
        bands = [shift_ref[j, pl.ds(g * 16, 16), :] for j in range(ORDERS)]
        first = 0
        held = None
        for i in range(ORDERS):
            sums = [None] * 6
            for j in range(ORDERS - i):
                c = [coef_ref[v, (first + j) * 6 + p] for p in range(6)]
                flat = c[0] + ty * (c[2] + ty * c[5])
                slope = c[1] + ty * c[4]
                for part in range(2):
                    band = bands[j][:, part * 128 : (part + 1) * 128]
                    for q, weight in enumerate((flat, slope, c[3])):
                        term = weight * band
                        at = q * 2 + part
                        sums[at] = term if sums[at] is None else sums[at] + term
            first += ORDERS - i
            ends = []
            for q in range(3):
                down_ref[0, pl.ds(q * SIDE + g * 16, 16), i * 128 : (i + 1) * 128] = sums[
                    q * 2
                ].astype(bf16)
                ends.append(sums[q * 2 + 1] + pltpu.roll(sums[q * 2 + 1], 64, 1))
            if i % 2 == 0:
                held = ends
            else:
                at = ORDERS * 128 + (i // 2) * 128
                for q in range(3):
                    down_ref[0, pl.ds(q * SIDE + g * 16, 16), at : at + 128] = jnp.where(
                        left, held[q], ends[q]
                    ).astype(bf16)
        return 0

    lax.fori_loop(0, SIDE // 16, step, 0)


def model_kernel(
    rows_ref, across_ref, down_ref, colf_ref, rowf_ref, sci_ref,
    diff_ref, score_ref, part_ref, top_ref, bot_ref, wide_ref, win_ref, stack_ref,
):
    v = pl.program_id(0)

    @pl.when(v == 0)
    def _():
        wide_ref[...] = rows_ref[...].reshape(GROUP * PICKPAD, 128).astype(f32)
        for slot in range(3):
            for n in range(VISITS):
                for b in range(3):
                    win_ref[n, slot * GROUP : (slot + 1) * GROUP, b * 128 : (b + 1) * 128] = (
                        wide_ref[pl.ds(slot * 18 + n * 3 + b, GROUP, stride=PICKPAD), :]
                    ).astype(bf16)

    for xb in range(2):
        at = xb * 128
        got = jnp.dot(
            win_ref[v, :, at : at + 256], across_ref[0], preferred_element_type=f32
        ).astype(bf16)
        for i in range(ORDERS):
            piece = got[:, i * 128 : (i + 1) * 128]
            stack_ref[i * 128 : (i + 1) * 128, at : at + 128] = piece[0:128]
            low = ORDERS * 128 + i * 64
            stack_ref[low : low + 64, at : at + 128] = piece[128:192]
    parts = jnp.dot(down_ref[0], stack_ref[...], preferred_element_type=f32)
    col = lax.broadcasted_iota(jnp.int32, (SIDE, COLS), 1).astype(f32)
    tx = (2.0 * col + 1.0) / COLS - 1.0
    model = parts[0:128] + tx * (parts[128:256] + tx * parts[256:384])
    diff = (sci_ref[0].astype(f32) - model).astype(bf16)
    diff_ref[0] = diff
    filt = jnp.dot(diff, colf_ref[0], preferred_element_type=f32).astype(bf16)
    top_ref[0] = filt[0:HALO]
    bot_ref[0] = filt[SIDE - HALO :]
    score = jnp.dot(rowf_ref[0, :, 0:128], filt, preferred_element_type=f32)
    score_ref[0] = score
    part_ref[0, 0:HALO] = score[0:HALO]
    part_ref[0, HALO:] = score[SIDE - HALO :]


def edge_kernel(part_ref, above_ref, below_ref, rowf_ref, _, score_ref, buf_ref, sem):
    for v in range(VISITS):
        gap = jnp.zeros((128 - 2 * HALO, COLS), bf16)
        ring = jnp.concatenate([below_ref[v], gap, above_ref[v]], axis=0)
        band = jnp.concatenate(
            [rowf_ref[v, 0:HALO, 128:256], rowf_ref[v, SIDE - HALO :, 128:256]], axis=0
        )
        buf_ref[v] = part_ref[v] + jnp.dot(band, ring, preferred_element_type=f32)
    top = pltpu.make_async_copy(buf_ref.at[:, 0:HALO], score_ref.at[:, 0:HALO], sem.at[0])
    bot = pltpu.make_async_copy(
        buf_ref.at[:, HALO : 2 * HALO], score_ref.at[:, SIDE - HALO : SIDE], sem.at[1]
    )
    top.start()
    bot.start()
    top.wait()
    bot.wait()


def sds(shape, dtype):
    return jax.ShapeDtypeStruct(shape, dtype)


def body(
    science, templates, cell_owner, cell_index, row_offset, col_offset, coefficients, psf_taps
):
    oy = row_offset[:, 0]
    ox = col_offset[:, 0]
    me = lax.axis_index("sky").astype(jnp.int32).reshape(1)
    info = jnp.pad(
        jnp.concatenate([cell_owner[0, :, 0], cell_index[0], oy]), (0, 128 - 78)
    ).astype(bf16)[None, :]

    packed = pl.pallas_call(
        pack_kernel,
        out_shape=sds((GROUP, PACKED, 128), bf16),
        in_specs=[VM, VM],
        out_specs=VM,
        scratch_shapes=[pltpu.VMEM((CELLS * SIDE, 128), f32)],
        name="pack",
    )(templates, info)
    stripes = lax.all_to_all(packed, "sky", 0, 0, tiled=True)

    taps = hermite_table()
    ahead = np.zeros((8, FAR), np.float32)
    ahead[:ORDERS, :TAPS] = taps
    back = np.zeros((8, FAR), np.float32)
    for u in range(TAPS):
        back[:ORDERS, (-MAXOFF - u) % FAR] = taps[:, u]
    psf = psf_taps.astype(f32)
    zero = jnp.zeros((VISITS, FAR - TAPS), f32)
    colrow = jnp.concatenate([jnp.flip(psf[:, 1], axis=1), zero], axis=1)
    rowrow = jnp.concatenate([psf[:, 0], zero], axis=1)
    psf_rows = jnp.stack([jnp.roll(colrow, -RAD, axis=1), jnp.roll(rowrow, -RAD, axis=1)], axis=1)

    across, down, colf, rowf = pl.pallas_call(
        bands_kernel,
        grid=(VISITS,),
        in_specs=[
            SM, SM, SM,
            pl.BlockSpec((8, FAR), lambda v: (0, 0)),
            pl.BlockSpec((8, FAR), lambda v: (0, 0)),
            pl.BlockSpec((1, 2, FAR), lambda v: (v, 0, 0)),
        ],
        out_specs=[
            pl.BlockSpec((1, FAR, 768), lambda v: (v, 0, 0)),
            pl.BlockSpec((1, 384, 1152), lambda v: (v, 0, 0)),
            pl.BlockSpec((1, COLS, COLS), lambda v: (v, 0, 0)),
            pl.BlockSpec((1, SIDE, FAR), lambda v: (v, 0, 0)),
        ],
        out_shape=[
            sds((VISITS, FAR, 768), bf16),
            sds((VISITS, 384, 1152), bf16),
            sds((VISITS, COLS, COLS), bf16),
            sds((VISITS, SIDE, FAR), bf16),
        ],
        scratch_shapes=[
            pltpu.VMEM((ORDERS, 360, 128), f32),
            pltpu.VMEM((ORDERS, SIDE, FAR), f32),
            pltpu.VMEM((ORDERS, SIDE, FAR), f32),
        ],
        name="bands",
    )(oy, ox, coefficients.reshape(VISITS, 126), jnp.asarray(ahead), jnp.asarray(back), psf_rows)

    picked = pl.pallas_call(
        select_kernel,
        out_shape=sds((GROUP, PICKPAD, 128), bf16),
        in_specs=[SM, VM, VM],
        out_specs=VM,
        name="select",
    )(me, stripes, jnp.asarray(request_selector()).astype(bf16))
    rows = lax.all_to_all(picked, "sky", 0, 0, tiled=True)

    difference, score, part, top, bot = pl.pallas_call(
        model_kernel,
        grid=(VISITS,),
        in_specs=[
            pl.BlockSpec((GROUP, PICKPAD, 128), lambda v: (0, 0, 0)),
            pl.BlockSpec((1, FAR, 768), lambda v: (v, 0, 0)),
            pl.BlockSpec((1, 384, 1152), lambda v: (v, 0, 0)),
            pl.BlockSpec((1, COLS, COLS), lambda v: (v, 0, 0)),
            pl.BlockSpec((1, SIDE, FAR), lambda v: (v, 0, 0)),
            pl.BlockSpec((1, SIDE, COLS), lambda v: (v, 0, 0)),
        ],
        out_specs=[
            pl.BlockSpec((1, SIDE, COLS), lambda v: (v, 0, 0)),
            pl.BlockSpec((1, SIDE, COLS), lambda v: (v, 0, 0)),
            pl.BlockSpec((1, 2 * HALO, COLS), lambda v: (v, 0, 0)),
            pl.BlockSpec((1, HALO, COLS), lambda v: (v, 0, 0)),
            pl.BlockSpec((1, HALO, COLS), lambda v: (v, 0, 0)),
        ],
        out_shape=[
            sds((VISITS, SIDE, COLS), bf16),
            sds((VISITS, SIDE, COLS), f32),
            sds((VISITS, 2 * HALO, COLS), f32),
            sds((VISITS, HALO, COLS), bf16),
            sds((VISITS, HALO, COLS), bf16),
        ],
        scratch_shapes=[
            pltpu.VMEM((GROUP * PICKPAD, 128), f32),
            pltpu.VMEM((VISITS, 192, 384), bf16),
            pltpu.VMEM((1152, COLS), bf16),
        ],
        name="model",
    )(rows, across, down, colf, rowf, science)

    count = lax.axis_size("ccd")
    above = lax.ppermute(bot, "ccd", [(i, i + 1) for i in range(count - 1)])
    below = lax.ppermute(top, "ccd", [(i + 1, i) for i in range(count - 1)])
    score = pl.pallas_call(
        edge_kernel,
        out_shape=sds((VISITS, SIDE, COLS), f32),
        in_specs=[VM, VM, VM, VM, pl.BlockSpec(memory_space=pl.ANY)],
        out_specs=pl.BlockSpec(memory_space=pl.ANY),
        scratch_shapes=[pltpu.VMEM((VISITS, 2 * HALO, COLS), f32), pltpu.SemaphoreType.DMA((2,))],
        input_output_aliases={4: 0},
        name="edges",
    )(part, above, below, rowf, score)
    return difference, score


def solution(mesh):
    in_specs = (
        P("sky", "ccd", None),
        P("sky", "ccd", None),
        P("sky", "ccd", None),
        P("sky", "ccd"),
        P("sky", "ccd"),
        P("sky", "ccd"),
        P("sky", "ccd", None, None),
        P("sky", None, None),
    )
    out_specs = (P("sky", "ccd", None), P("sky", "ccd", None))
    return jax.shard_map(body, mesh=mesh, in_specs=in_specs, out_specs=out_specs, check_vma=False)
```

```python
import jax
import jax.numpy as jnp
import numpy as np
from jax import lax
from jax.experimental import pallas as pl
from jax.experimental.pallas import tpu as pltpu
from jax.sharding import PartitionSpec as P

RAD = 15
TAPS = 31
ORDERS = 6
GROUP = 64
CELLS = 16
SIDE = 128
VISITS = 6
COLS = 256
HALO = 16
STRIPE = 32
PACKED = 40
PICKS = 40
LONG = 1024
MAXOFF = 98
FAR = 256
f32 = jnp.float32
bf16 = jnp.bfloat16
VM = pl.BlockSpec(memory_space=pltpu.VMEM)
HB = pl.BlockSpec(memory_space=pltpu.HBM)
SM = pl.BlockSpec(memory_space=pltpu.SMEM)
LIMIT = pltpu.CompilerParams(vmem_limit_bytes=32 * 2**20)


def hermite_table():
    t = (np.arange(TAPS, dtype=np.float32) - np.float32(RAD)) / np.float32(4.0)
    series = [np.ones(t.shape, np.float32), np.float32(2.0) * t]
    for n in range(1, ORDERS - 1):
        series.append(np.float32(2.0) * t * series[n] - np.float32(2.0 * n) * series[n - 1])
    w = np.stack(series) * np.exp(np.float32(-0.5) * t * t)
    w = w / np.sqrt(np.sum(w * w, axis=1, keepdims=True))
    return np.asarray(w, dtype=jnp.bfloat16).astype(np.float32)


def quarter(x, k):
    return pltpu.roll(x, (k % 4) * 32, 1) if k % 4 else x


def choose(quarters, *items):
    out = items[-1]
    for mask, item in zip(quarters, items[:-1]):
        out = jnp.where(mask, item, out)
    return out


def quarter_masks(count):
    at = lax.broadcasted_iota(jnp.int32, (count, 128), 1) // 32
    return [at == k for k in range(3)]


def transpose_quarters(items, masks):
    turned = [quarter(x, j) for j, x in enumerate(items)]
    return [
        quarter(choose(masks, *(turned[(m - t) % 4] for m in range(4))), -t) for t in range(4)
    ]


def across_band(taps):
    band = np.zeros((FAR, ORDERS * 128), np.float32)
    for i in range(ORDERS):
        for x in range(128):
            band[x : x + TAPS, i * 128 + x] = taps[i]
    return band


def scatter_rows():
    r = lax.broadcasted_iota(jnp.int32, (256, 256), 0)
    c = lax.broadcasted_iota(jnp.int32, (256, 256), 1)
    return jnp.where(c == (r % 8) * 32 + r // 8, 1.0, 0.0).astype(bf16)


def gather_rows():
    r = lax.broadcasted_iota(jnp.int32, (256, 256), 0)
    c = lax.broadcasted_iota(jnp.int32, (256, 256), 1)
    source = ((r % 16) * 2 + (r // 16) % 2) * 8 + r // 32
    return jnp.where(c == source, 1.0, 0.0).astype(bf16)


def pack_kernel(
    cells_any, owner_any, index_any, oy_any, ox_any, out_ref,
    cells_ref, owner_ref, index_ref, oy_ref, ox_ref, info_ref, sem,
):
    copies = [
        pltpu.make_async_copy(src, dst, sem.at[k])
        for k, (src, dst) in enumerate(
            (
                (cells_any, cells_ref), (owner_any, owner_ref), (index_any, index_ref),
                (oy_any, oy_ref), (ox_any, ox_ref),
            )
        )
    ]
    for copy in copies:
        copy.start()
    move = scatter_rows()
    masks = quarter_masks(256)
    info_ref[...] = jnp.zeros((8, 128), f32)
    for copy in copies[1:]:
        copy.wait()
    info_ref[0:1, 0:36] = owner_ref[...].astype(f32)
    info_ref[1:2, 0:36] = index_ref[...].astype(f32)
    info_ref[2:3, 0:VISITS] = oy_ref[...].astype(f32)
    info_ref[3:4, 0:VISITS] = ox_ref[...].astype(f32)
    info = info_ref[...].astype(bf16)
    for d in range(GROUP):
        out_ref[d // 2, d % 2, STRIPE:PACKED, :] = info
    copies[0].wait()
    moved = []
    for q in range(4):
        halves = [
            cells_ref[h * 8 : (h + 1) * 8, q * 32 : (q + 1) * 32, :].reshape(256, 128)
            for h in range(2)
        ]
        moved.append(
            jnp.dot(move, jnp.concatenate(halves, axis=1), preferred_element_type=f32)
        )
    for h in range(2):
        groups = transpose_quarters([m[:, h * 128 : (h + 1) * 128] for m in moved], masks)
        for c in range(2):
            for u in range(2):
                at = u * CELLS + h * 8
                out_ref[:, c, at : at + 8, :] = groups[c + 2 * u].reshape(32, 8, 128).astype(bf16)


def select_kernel(me_ref, stripes_ref, out_ref, asks_ref):
    table = jnp.concatenate(
        [
            stripes_ref[:, 0:CELLS, :].reshape(GROUP * CELLS, 128),
            stripes_ref[:, CELLS:STRIPE, :].reshape(GROUP * CELLS, 128),
        ],
        axis=1,
    )
    me = me_ref[0]
    own = (me // 2).astype(f32)
    core = (me % 2).astype(f32)
    for n in range(GROUP):
        asks_ref[:, n, :] = stripes_ref[n, STRIPE:PACKED, :].astype(f32)
    ids = asks_ref[0] * CELLS + asks_ref[1]
    tops = asks_ref[2]
    lefts = asks_ref[3]
    lane = lax.broadcasted_iota(jnp.int32, (GROUP, 128), 1)
    number = [(lane + 128 * k).astype(f32) for k in range(GROUP * CELLS // 128)]
    first = (lane // 32 * 32).astype(f32) + own
    masks = quarter_masks(GROUP)
    move = scatter_rows()

    def column(x, k):
        return jnp.broadcast_to(x[:, k : k + 1], (GROUP, 128))

    lines, last = [], []
    fifths = []
    for v in range(VISITS):
        hot = []
        for r in range(6):
            want = column(ids, v * 6 + r)
            hot.append(
                jnp.concatenate(
                    [jnp.where(n == want, 1.0, 0.0).astype(bf16) for n in number], axis=1
                )
            )
        got = jnp.dot(jnp.concatenate(hot, axis=0), table, preferred_element_type=f32)
        above = first >= column(tops, v)
        late = column(lefts, v) >= 32.0 * (core + 1.0)
        whole, fifth = [], []
        for b in range(3):
            for u in range(2):
                upper = got[b * GROUP : (b + 1) * GROUP, u * 128 : (u + 1) * 128]
                lower = got[(3 + b) * GROUP : (4 + b) * GROUP, u * 128 : (u + 1) * 128]
                whole.append(jnp.where(above, upper, quarter(lower, -1)))
                fifth.append(lower)
        whole[0] = jnp.where(late, whole[5], whole[0])
        fifth[0] = jnp.where(late, fifth[5], fifth[0])
        lines += [w.astype(bf16) for w in whole[:5]]
        fifths.append(choose(masks, *(quarter(fifth[k], k) for k in range(4))).astype(bf16))
        last.append(quarter(fifth[4], v))
    lines += fifths
    lines.append(choose(masks, *last[:4]).astype(bf16))
    lines.append(choose(masks, last[4], last[5], last[5], last[5]).astype(bf16))
    lines += [lines[-1], lines[-1]]
    for k in range(PICKS // 8):
        block = jnp.concatenate(
            [
                jnp.concatenate([x[h * 32 : (h + 1) * 32] for x in lines[k * 8 : k * 8 + 8]], axis=0)
                for h in range(2)
            ],
            axis=1,
        )
        moved = jnp.dot(move, block, preferred_element_type=f32)
        for h in range(2):
            out_ref[h * 32 : (h + 1) * 32, k * 8 : k * 8 + 8, :] = (
                moved[:, h * 128 : (h + 1) * 128].reshape(32, 8, 128).astype(bf16)
            )


def bands_kernel(
    oy_ref, coef_ref, taps_ref, psf_ref, down_ref, colf_ref, rowf_ref, toep_ref, shift_ref,
):
    v = pl.program_id(0)

    def spread(row, count):
        return pltpu.roll(jnp.broadcast_to(row, (count, FAR)), 0, 1, stride=1, stride_axis=0)

    @pl.when(v == 0)
    def _():
        for i in range(ORDERS):
            toep_ref[i] = spread(taps_ref[i : i + 1, :], SIDE)

    oy = oy_ref[v]
    for i in range(ORDERS):
        shift_ref[i] = pltpu.roll(toep_ref[i], oy, 1)
    near = lax.broadcasted_iota(jnp.int32, (COLS, COLS), 0) - lax.broadcasted_iota(
        jnp.int32, (COLS, COLS), 1
    )
    colf_ref[0] = jnp.where(
        jnp.abs(near) <= RAD, spread(psf_ref[0, 0:1, :], COLS), 0.0
    ).astype(bf16)
    rowf_ref[0] = spread(psf_ref[0, 1:2, :], SIDE).astype(bf16)

    masks = quarter_masks(16)
    three = lax.broadcasted_iota(jnp.int32, (16, 128), 1) < 96

    def step(g, _):
        row = lax.broadcasted_iota(jnp.int32, (16, 128), 0) + g * 16
        ty = (2.0 * row.astype(f32) + 1.0) / SIDE - 1.0
        bands = [shift_ref[j, pl.ds(g * 16, 16), :] for j in range(ORDERS)]
        first = 0
        fifth = []
        for i in range(ORDERS):
            sums = [None] * 6
            for j in range(ORDERS - i):
                c = [coef_ref[v, (first + j) * 6 + p] for p in range(6)]
                flat = c[0] + ty * (c[2] + ty * c[5])
                slope = c[1] + ty * c[4]
                for part in range(2):
                    band = bands[j][:, part * 128 : (part + 1) * 128]
                    for q, weight in enumerate((flat, slope, c[3])):
                        term = weight * band
                        at = q * 2 + part
                        sums[at] = term if sums[at] is None else sums[at] + term
            first += ORDERS - i
            ends = []
            for q in range(3):
                low, high = sums[q * 2], sums[q * 2 + 1]
                down_ref[0, pl.ds(q * SIDE + g * 16, 16), i * 128 : (i + 1) * 128] = (
                    low + jnp.where(three, quarter(high, -1), 0.0)
                ).astype(bf16)
                ends.append(quarter(high, i))
            fifth.append(ends)
        for q in range(3):
            row_at = pl.ds(q * SIDE + g * 16, 16)
            down_ref[0, row_at, 768:896] = choose(masks, *(fifth[i][q] for i in range(4))).astype(
                bf16
            )
            gap = jnp.zeros((16, 128), f32)
            down_ref[0, row_at, 896:1024] = choose(
                masks, fifth[4][q], fifth[5][q], gap, gap
            ).astype(bf16)
        return 0

    lax.fori_loop(0, SIDE // 16, step, 0)


def model_kernel(
    ox_ref, rows_ref, across_any, down_any, colf_any, rowf_any, sci_any,
    diff_any, score_any, part_ref, top_ref, bot_ref,
    across_ref, down_ref, colf_ref, rowf_ref, sci_ref, diff_ref, score_ref,
    win_ref, stack_ref, sem, out_sem,
):
    band = pltpu.make_async_copy(across_any, across_ref, sem.at[VISITS, 0])
    band.start()
    fetch = [
        [
            pltpu.make_async_copy(src.at[v], dst.at[v], sem.at[v, k])
            for k, (src, dst) in enumerate(
                ((down_any, down_ref), (colf_any, colf_ref), (rowf_any, rowf_ref), (sci_any, sci_ref))
            )
        ]
        for v in range(VISITS)
    ]
    for copies in fetch:
        for copy in copies:
            copy.start()
    half = GROUP // 2
    move = gather_rows()
    masks = quarter_masks(half)
    lane = lax.broadcasted_iota(jnp.int32, (160, 128), 1)
    lines = []
    for k in range(PICKS // 8):
        block = jnp.concatenate(
            [
                rows_ref[h * 32 : (h + 1) * 32, k * 8 : k * 8 + 8, :].reshape(256, 128)
                for h in range(2)
            ],
            axis=1,
        )
        lines.append(jnp.dot(move, block, preferred_element_type=f32))

    def take(row, c):
        at = (row % 8) * 32 + c * 16
        return jnp.concatenate(
            [lines[row // 8][at : at + 16, h * 128 : (h + 1) * 128] for h in range(2)], axis=0
        )

    def window(v):
        groups = [[take(v * 5 + k, c) for c in range(2)] for k in range(5)]
        blocks = [
            transpose_quarters(
                [groups[k][0], groups[k][1], groups[m][0], groups[m][1]], masks
            )
            for k, m in ((0, 1), (2, 3), (4, 0))
        ]
        e = [take(30 + v, c) for c in range(2)]
        f = [take(36 + v // 4, c) for c in range(2)]
        fifths = [
            choose(masks, e[0], quarter(e[1], 1), quarter(e[0], 1), quarter(e[1], 2)),
            choose(masks, quarter(e[0], 2), quarter(e[1], 3), quarter(e[0], 3), e[1]),
            choose(
                masks, quarter(f[0], -v), quarter(f[1], 1 - v), quarter(e[0], 2), quarter(e[1], 3)
            ),
        ]
        back = 128 - ox_ref[v]
        turned = [
            pltpu.roll(jnp.concatenate(blocks[b] + [fifths[b]], axis=0), back, 1)
            for b in range(3)
        ]
        tiles = [
            jnp.where(lane < back, turned[b], turned[min(b + 1, 2)]).astype(bf16) for b in range(3)
        ]
        for xb in range(2):
            at = v * 320 + xb * 160
            win_ref[at : at + 160, 0:128] = tiles[xb]
            win_ref[at : at + 160, 128:256] = tiles[xb + 1]

    col = lax.broadcasted_iota(jnp.int32, (SIDE, COLS), 1).astype(f32)
    tx = (2.0 * col + 1.0) / COLS - 1.0
    out = []

    def spread(group):
        at = group[0] * 320
        got = jnp.dot(
            win_ref[at : at + 320 * len(group), :], across_ref[...], preferred_element_type=f32
        ).astype(bf16)
        for n, v in enumerate(group):
            stack_ref[v, 960:LONG, :] = jnp.zeros((LONG - 960, COLS), bf16)
            for xb in range(2):
                row = n * 320 + xb * 160
                for i in range(ORDERS):
                    piece = got[row : row + 160, i * 128 : (i + 1) * 128]
                    low = ORDERS * 128 + i * half
                    cols = slice(xb * 128, (xb + 1) * 128)
                    stack_ref[v, i * 128 : (i + 1) * 128, cols] = piece[0:128]
                    stack_ref[v, low : low + half, cols] = piece[128:160]

    def finish(v):
        parts = jnp.dot(down_ref[v], stack_ref[v], preferred_element_type=f32)
        model = parts[0:128] + tx * (parts[128:256] + tx * parts[256:384])
        diff = (sci_ref[v].astype(f32) - model).astype(bf16)
        diff_ref[v] = diff
        filt = jnp.dot(diff, colf_ref[v], preferred_element_type=f32).astype(bf16)
        top_ref[v] = filt[0:HALO]
        bot_ref[v] = filt[SIDE - HALO :]
        score = jnp.dot(rowf_ref[v, :, 0:128], filt, preferred_element_type=f32)
        score_ref[v] = score
        part_ref[v, 0:HALO] = score[0:HALO]
        part_ref[v, HALO:] = score[SIDE - HALO :]
        out.append(pltpu.make_async_copy(diff_ref.at[v], diff_any.at[v], out_sem.at[v, 0]))
        out.append(pltpu.make_async_copy(score_ref.at[v], score_any.at[v], out_sem.at[v, 1]))
        out[-2].start()
        out[-1].start()

    early, rest = (0, 1, 2), (3, 4, 5)
    for v in early:
        window(v)
    band.wait()
    spread(early)
    for v in rest:
        window(v)
    for v in early:
        for copy in fetch[v]:
            copy.wait()
    spread(rest)
    for v in early:
        finish(v)
    for v in rest:
        for copy in fetch[v]:
            copy.wait()
    for v in rest:
        finish(v)
    for copy in out:
        copy.wait()


def edge_kernel(part_ref, above_ref, below_ref, rowf_ref, _, score_ref, buf_ref, sem):
    for v in range(VISITS):
        gap = jnp.zeros((128 - 2 * HALO, COLS), bf16)
        ring = jnp.concatenate([below_ref[v], gap, above_ref[v]], axis=0)
        band = jnp.concatenate(
            [rowf_ref[v, 0:HALO, 128:256], rowf_ref[v, SIDE - HALO :, 128:256]], axis=0
        )
        buf_ref[v] = part_ref[v] + jnp.dot(band, ring, preferred_element_type=f32)
    top = pltpu.make_async_copy(buf_ref.at[:, 0:HALO], score_ref.at[:, 0:HALO], sem.at[0])
    bot = pltpu.make_async_copy(
        buf_ref.at[:, HALO : 2 * HALO], score_ref.at[:, SIDE - HALO : SIDE], sem.at[1]
    )
    top.start()
    bot.start()
    top.wait()
    bot.wait()


def sds(shape, dtype):
    return jax.ShapeDtypeStruct(shape, dtype)


def near(x):
    return pltpu.with_memory_space_constraint(x, pltpu.VMEM)


def body(
    science, templates, cell_owner, cell_index, row_offset, col_offset, coefficients, psf_taps
):
    oy = row_offset[:, 0]
    ox = col_offset[:, 0]
    me = lax.axis_index("sky").astype(jnp.int32).reshape(1)

    packed = pl.pallas_call(
        pack_kernel,
        out_shape=sds((GROUP // 2, 2, PACKED, 128), bf16),
        in_specs=[HB] * 5,
        out_specs=VM,
        scratch_shapes=[
            pltpu.VMEM((CELLS, SIDE, 128), bf16),
            pltpu.VMEM((1, 36), jnp.int32),
            pltpu.VMEM((1, 36), jnp.int32),
            pltpu.VMEM((1, VISITS), jnp.int32),
            pltpu.VMEM((1, VISITS), jnp.int32),
            pltpu.VMEM((8, 128), f32),
            pltpu.SemaphoreType.DMA((5,)),
        ],
        name="pack",
    )(templates, cell_owner.reshape(1, 36), cell_index, oy.reshape(1, 6), ox.reshape(1, 6))
    stripes = lax.all_to_all(packed.reshape(GROUP, PACKED, 128), "sky", 0, 0, tiled=True)

    taps = hermite_table()
    ahead = np.zeros((8, FAR), np.float32)
    ahead[:ORDERS, :TAPS] = taps
    psf = psf_taps.astype(f32)
    zero = jnp.zeros((VISITS, FAR - TAPS), f32)
    colrow = jnp.concatenate([jnp.flip(psf[:, 1], axis=1), zero], axis=1)
    rowrow = jnp.concatenate([psf[:, 0], zero], axis=1)
    psf_rows = jnp.stack([jnp.roll(colrow, -RAD, axis=1), jnp.roll(rowrow, -RAD, axis=1)], axis=1)

    down, colf, rowf = pl.pallas_call(
        bands_kernel,
        grid=(VISITS,),
        in_specs=[
            SM, SM,
            pl.BlockSpec((8, FAR), lambda v: (0, 0)),
            pl.BlockSpec((1, 2, FAR), lambda v: (v, 0, 0)),
        ],
        out_specs=[
            pl.BlockSpec((1, 384, LONG), lambda v: (v, 0, 0)),
            pl.BlockSpec((1, COLS, COLS), lambda v: (v, 0, 0)),
            pl.BlockSpec((1, SIDE, FAR), lambda v: (v, 0, 0)),
        ],
        out_shape=[
            sds((VISITS, 384, LONG), bf16),
            sds((VISITS, COLS, COLS), bf16),
            sds((VISITS, SIDE, FAR), bf16),
        ],
        scratch_shapes=[
            pltpu.VMEM((ORDERS, SIDE, FAR), f32),
            pltpu.VMEM((ORDERS, SIDE, FAR), f32),
        ],
        name="bands",
    )(oy, coefficients.reshape(VISITS, 126), jnp.asarray(ahead), psf_rows)
    stripes, down = lax.optimization_barrier((stripes, down))

    picked = pl.pallas_call(
        select_kernel,
        out_shape=sds((GROUP, PICKS, 128), bf16),
        in_specs=[SM, VM],
        out_specs=VM,
        scratch_shapes=[pltpu.VMEM((8, GROUP, 128), f32)],
        compiler_params=LIMIT,
        name="select",
    )(me, near(stripes))
    rows = lax.all_to_all(picked, "sky", 0, 0, tiled=True)

    difference, score, part, top, bot = pl.pallas_call(
        model_kernel,
        in_specs=[SM, VM] + [HB] * 5,
        out_specs=[HB, HB, VM, VM, VM],
        out_shape=[
            sds((VISITS, SIDE, COLS), bf16),
            sds((VISITS, SIDE, COLS), f32),
            pltpu.VMEM((VISITS, 2 * HALO, COLS), f32),
            sds((VISITS, HALO, COLS), bf16),
            sds((VISITS, HALO, COLS), bf16),
        ],
        scratch_shapes=[
            pltpu.VMEM((FAR, 768), bf16),
            pltpu.VMEM((VISITS, 384, LONG), bf16),
            pltpu.VMEM((VISITS, COLS, COLS), bf16),
            pltpu.VMEM((VISITS, SIDE, FAR), bf16),
            pltpu.VMEM((VISITS, SIDE, COLS), bf16),
            pltpu.VMEM((VISITS, SIDE, COLS), bf16),
            pltpu.VMEM((VISITS, SIDE, COLS), f32),
            pltpu.VMEM((VISITS * 320, 256), bf16),
            pltpu.VMEM((VISITS, LONG, COLS), bf16),
            pltpu.SemaphoreType.DMA((VISITS + 1, 4)),
            pltpu.SemaphoreType.DMA((VISITS, 2)),
        ],
        name="model",
    )(ox, near(rows), jnp.asarray(across_band(taps)).astype(bf16), down, colf, rowf, science)

    count = lax.axis_size("ccd")
    above = lax.ppermute(bot, "ccd", [(i, i + 1) for i in range(count - 1)])
    below = lax.ppermute(top, "ccd", [(i + 1, i) for i in range(count - 1)])
    score = pl.pallas_call(
        edge_kernel,
        out_shape=sds((VISITS, SIDE, COLS), f32),
        in_specs=[VM, VM, VM, VM, pl.BlockSpec(memory_space=pl.ANY)],
        out_specs=pl.BlockSpec(memory_space=pl.ANY),
        scratch_shapes=[pltpu.VMEM((VISITS, 2 * HALO, COLS), f32), pltpu.SemaphoreType.DMA((2,))],
        input_output_aliases={4: 0},
        compiler_params=LIMIT,
        name="edges",
    )(part, near(above), near(below), rowf, score)
    return difference, score


def solution(mesh):
    in_specs = (
        P("sky", "ccd", None),
        P("sky", "ccd", None),
        P("sky", "ccd", None),
        P("sky", "ccd"),
        P("sky", "ccd"),
        P("sky", "ccd"),
        P("sky", "ccd", None, None),
        P("sky", None, None),
    )
    out_specs = (P("sky", "ccd", None), P("sky", "ccd", None))
    return jax.shard_map(body, mesh=mesh, in_specs=in_specs, out_specs=out_specs, check_vma=False)
```

```python
import jax
import jax.numpy as jnp
import numpy as np
from jax import lax
from jax.experimental import pallas as pl
from jax.experimental.pallas import tpu as pltpu
from jax.sharding import PartitionSpec as P

RAD = 15
TAPS = 31
ORDERS = 6
GROUP = 64
CELLS = 16
SIDE = 128
VISITS = 6
COLS = 256
HALO = 16
STRIPE = 32
PACKED = 40
PICKS = 40
LONG = 1024
MAXOFF = 98
FAR = 256
f32 = jnp.float32
bf16 = jnp.bfloat16
VM = pl.BlockSpec(memory_space=pltpu.VMEM)
HB = pl.BlockSpec(memory_space=pltpu.HBM)
SM = pl.BlockSpec(memory_space=pltpu.SMEM)
LIMIT = pltpu.CompilerParams(vmem_limit_bytes=32 * 2**20)


def hermite_table():
    t = (np.arange(TAPS, dtype=np.float32) - np.float32(RAD)) / np.float32(4.0)
    series = [np.ones(t.shape, np.float32), np.float32(2.0) * t]
    for n in range(1, ORDERS - 1):
        series.append(np.float32(2.0) * t * series[n] - np.float32(2.0 * n) * series[n - 1])
    w = np.stack(series) * np.exp(np.float32(-0.5) * t * t)
    w = w / np.sqrt(np.sum(w * w, axis=1, keepdims=True))
    return np.asarray(w, dtype=jnp.bfloat16).astype(np.float32)


def quarter(x, k):
    return pltpu.roll(x, (k % 4) * 32, 1) if k % 4 else x


def choose(quarters, *items):
    out = items[-1]
    for mask, item in zip(quarters, items[:-1]):
        out = jnp.where(mask, item, out)
    return out


def quarter_masks(count):
    at = lax.broadcasted_iota(jnp.int32, (count, 128), 1) // 32
    return [at == k for k in range(3)]


def transpose_quarters(items, masks):
    turned = [quarter(x, j) for j, x in enumerate(items)]
    return [
        quarter(choose(masks, *(turned[(m - t) % 4] for m in range(4))), -t) for t in range(4)
    ]


def across_band(taps):
    band = np.zeros((FAR, ORDERS * 128), np.float32)
    for i in range(ORDERS):
        for x in range(128):
            band[x : x + TAPS, i * 128 + x] = taps[i]
    return band


def scatter_rows():
    r = lax.broadcasted_iota(jnp.int32, (256, 256), 0)
    c = lax.broadcasted_iota(jnp.int32, (256, 256), 1)
    return jnp.where(c == (r % 8) * 32 + r // 8, 1.0, 0.0).astype(bf16)


def gather_rows():
    r = lax.broadcasted_iota(jnp.int32, (256, 256), 0)
    c = lax.broadcasted_iota(jnp.int32, (256, 256), 1)
    source = ((r % 16) * 2 + (r // 16) % 2) * 8 + r // 32
    return jnp.where(c == source, 1.0, 0.0).astype(bf16)


def pack_kernel(
    cells_any, owner_any, index_any, oy_any, ox_any, out_ref,
    cells_ref, owner_ref, index_ref, oy_ref, ox_ref, info_ref, sem,
):
    copies = [
        pltpu.make_async_copy(src, dst, sem.at[k])
        for k, (src, dst) in enumerate(
            (
                (cells_any, cells_ref), (owner_any, owner_ref), (index_any, index_ref),
                (oy_any, oy_ref), (ox_any, ox_ref),
            )
        )
    ]
    for copy in copies:
        copy.start()
    move = scatter_rows()
    masks = quarter_masks(256)
    info_ref[...] = jnp.zeros((8, 128), f32)
    for copy in copies[1:]:
        copy.wait()
    info_ref[0:1, 0:36] = owner_ref[...].astype(f32)
    info_ref[1:2, 0:36] = index_ref[...].astype(f32)
    info_ref[2:3, 0:VISITS] = oy_ref[...].astype(f32)
    info_ref[3:4, 0:VISITS] = ox_ref[...].astype(f32)
    info = info_ref[...].astype(bf16)
    for d in range(GROUP):
        out_ref[d // 2, d % 2, STRIPE:PACKED, :] = info
    copies[0].wait()
    moved = []
    for q in range(4):
        halves = [
            cells_ref[h * 8 : (h + 1) * 8, q * 32 : (q + 1) * 32, :].reshape(256, 128)
            for h in range(2)
        ]
        moved.append(
            jnp.dot(move, jnp.concatenate(halves, axis=1), preferred_element_type=f32)
        )
    for h in range(2):
        groups = transpose_quarters([m[:, h * 128 : (h + 1) * 128] for m in moved], masks)
        for c in range(2):
            for u in range(2):
                at = u * CELLS + h * 8
                out_ref[:, c, at : at + 8, :] = groups[c + 2 * u].reshape(32, 8, 128).astype(bf16)


def select_kernel(me_ref, stripes_ref, out_ref, asks_ref):
    table = jnp.concatenate(
        [
            stripes_ref[:, 0:CELLS, :].reshape(GROUP * CELLS, 128),
            stripes_ref[:, CELLS:STRIPE, :].reshape(GROUP * CELLS, 128),
        ],
        axis=1,
    )
    me = me_ref[0]
    own = (me // 2).astype(f32)
    core = (me % 2).astype(f32)
    for n in range(GROUP):
        asks_ref[:, n, :] = stripes_ref[n, STRIPE:PACKED, :].astype(f32)
    ids = asks_ref[0] * CELLS + asks_ref[1]
    tops = asks_ref[2]
    lefts = asks_ref[3]
    lane = lax.broadcasted_iota(jnp.int32, (GROUP, 128), 1)
    number = [(lane + 128 * k).astype(f32) for k in range(GROUP * CELLS // 128)]
    first = (lane // 32 * 32).astype(f32) + own
    masks = quarter_masks(GROUP)
    move = scatter_rows()

    def column(x, k):
        return jnp.broadcast_to(x[:, k : k + 1], (GROUP, 128))

    lines, last = [], []
    fifths = []
    for v in range(VISITS):
        hot = []
        for r in range(6):
            want = column(ids, v * 6 + r)
            hot.append(
                jnp.concatenate(
                    [jnp.where(n == want, 1.0, 0.0).astype(bf16) for n in number], axis=1
                )
            )
        got = jnp.dot(jnp.concatenate(hot, axis=0), table, preferred_element_type=f32)
        above = first >= column(tops, v)
        late = column(lefts, v) >= 32.0 * (core + 1.0)
        whole, fifth = [], []
        for b in range(3):
            for u in range(2):
                upper = got[b * GROUP : (b + 1) * GROUP, u * 128 : (u + 1) * 128]
                lower = got[(3 + b) * GROUP : (4 + b) * GROUP, u * 128 : (u + 1) * 128]
                whole.append(jnp.where(above, upper, quarter(lower, -1)))
                fifth.append(lower)
        whole[0] = jnp.where(late, whole[5], whole[0])
        fifth[0] = jnp.where(late, fifth[5], fifth[0])
        lines += [w.astype(bf16) for w in whole[:5]]
        fifths.append(choose(masks, *(quarter(fifth[k], k) for k in range(4))).astype(bf16))
        last.append(quarter(fifth[4], v))
    lines += fifths
    lines.append(choose(masks, *last[:4]).astype(bf16))
    lines.append(choose(masks, last[4], last[5], last[5], last[5]).astype(bf16))
    lines += [lines[-1], lines[-1]]
    for k in range(PICKS // 8):
        block = jnp.concatenate(
            [
                jnp.concatenate([x[h * 32 : (h + 1) * 32] for x in lines[k * 8 : k * 8 + 8]], axis=0)
                for h in range(2)
            ],
            axis=1,
        )
        moved = jnp.dot(move, block, preferred_element_type=f32)
        for h in range(2):
            out_ref[h * 32 : (h + 1) * 32, k * 8 : k * 8 + 8, :] = (
                moved[:, h * 128 : (h + 1) * 128].reshape(32, 8, 128).astype(bf16)
            )


def bands_kernel(
    oy_ref, coef_ref, taps_ref, psf_ref,
    near_ref, far_ref, colf_ref, rowf_ref, down_ref, toep_ref, shift_ref,
):
    v = pl.program_id(0)

    def spread(row, count):
        return pltpu.roll(jnp.broadcast_to(row, (count, FAR)), 0, 1, stride=1, stride_axis=0)

    @pl.when(v == 0)
    def _():
        for i in range(ORDERS):
            toep_ref[i] = spread(taps_ref[i : i + 1, :], SIDE)

    oy = oy_ref[v]
    for i in range(ORDERS):
        shift_ref[i] = pltpu.roll(toep_ref[i], oy, 1)
    near = lax.broadcasted_iota(jnp.int32, (COLS, COLS), 0) - lax.broadcasted_iota(
        jnp.int32, (COLS, COLS), 1
    )
    colf_ref[0] = jnp.where(
        jnp.abs(near) <= RAD, spread(psf_ref[0, 0:1, :], COLS), 0.0
    ).astype(bf16)
    rowf_ref[0] = spread(psf_ref[0, 1:2, :], SIDE).astype(bf16)

    masks = quarter_masks(16)
    three = lax.broadcasted_iota(jnp.int32, (16, 128), 1) < 96

    def step(g, _):
        row = lax.broadcasted_iota(jnp.int32, (16, 128), 0) + g * 16
        ty = (2.0 * row.astype(f32) + 1.0) / SIDE - 1.0
        bands = [shift_ref[j, pl.ds(g * 16, 16), :] for j in range(ORDERS)]
        first = 0
        fifth = []
        for i in range(ORDERS):
            sums = [None] * 6
            for j in range(ORDERS - i):
                c = [coef_ref[v, (first + j) * 6 + p] for p in range(6)]
                flat = c[0] + ty * (c[2] + ty * c[5])
                slope = c[1] + ty * c[4]
                for part in range(2):
                    band = bands[j][:, part * 128 : (part + 1) * 128]
                    for q, weight in enumerate((flat, slope, c[3])):
                        term = weight * band
                        at = q * 2 + part
                        sums[at] = term if sums[at] is None else sums[at] + term
            first += ORDERS - i
            ends = []
            for q in range(3):
                low, high = sums[q * 2], sums[q * 2 + 1]
                down_ref[pl.ds(q * SIDE + g * 16, 16), i * 128 : (i + 1) * 128] = (
                    low + jnp.where(three, quarter(high, -1), 0.0)
                ).astype(bf16)
                ends.append(quarter(high, i))
            fifth.append(ends)
        for q in range(3):
            row_at = pl.ds(q * SIDE + g * 16, 16)
            down_ref[row_at, 768:896] = choose(masks, *(fifth[i][q] for i in range(4))).astype(
                bf16
            )
            gap = jnp.zeros((16, 128), f32)
            down_ref[row_at, 896:1024] = choose(
                masks, fifth[4][q], fifth[5][q], gap, gap
            ).astype(bf16)
        return 0

    lax.fori_loop(0, SIDE // 16, step, 0)

    @pl.when(v < 3)
    def _():
        near_ref[v] = down_ref[...]

    @pl.when(v >= 3)
    def _():
        far_ref[0] = down_ref[...]


def model_kernel(
    ox_ref, rows_ref, down_ref, across_any, far_any, colf_any, sci_any,
    diff_any, filt_any, top_ref, bot_ref,
    across_ref, far_ref, colf_ref, sci_ref, diff_ref, filt_ref, win_ref, stack_ref, sem, out_sem,
):
    whole = [
        pltpu.make_async_copy(src, dst, sem.at[k])
        for k, (src, dst) in enumerate(
            (
                (across_any, across_ref), (colf_any, colf_ref), (sci_any, sci_ref),
                (far_any, far_ref),
            )
        )
    ]
    for copy in whole:
        copy.start()
    half = GROUP // 2
    move = gather_rows()
    masks = quarter_masks(half)
    lane = lax.broadcasted_iota(jnp.int32, (160, 128), 1)
    lines = []
    for k in range(PICKS // 8):
        block = jnp.concatenate(
            [
                rows_ref[h * 32 : (h + 1) * 32, k * 8 : k * 8 + 8, :].reshape(256, 128)
                for h in range(2)
            ],
            axis=1,
        )
        lines.append(jnp.dot(move, block, preferred_element_type=f32))

    def take(row, c):
        at = (row % 8) * 32 + c * 16
        return jnp.concatenate(
            [lines[row // 8][at : at + 16, h * 128 : (h + 1) * 128] for h in range(2)], axis=0
        )

    def window(v):
        groups = [[take(v * 5 + k, c) for c in range(2)] for k in range(5)]
        blocks = [
            transpose_quarters(
                [groups[k][0], groups[k][1], groups[m][0], groups[m][1]], masks
            )
            for k, m in ((0, 1), (2, 3), (4, 0))
        ]
        e = [take(30 + v, c) for c in range(2)]
        f = [take(36 + v // 4, c) for c in range(2)]
        fifths = [
            choose(masks, e[0], quarter(e[1], 1), quarter(e[0], 1), quarter(e[1], 2)),
            choose(masks, quarter(e[0], 2), quarter(e[1], 3), quarter(e[0], 3), e[1]),
            choose(
                masks, quarter(f[0], -v), quarter(f[1], 1 - v), quarter(e[0], 2), quarter(e[1], 3)
            ),
        ]
        back = 128 - ox_ref[v]
        turned = [
            pltpu.roll(jnp.concatenate(blocks[b] + [fifths[b]], axis=0), back, 1)
            for b in range(3)
        ]
        tiles = [
            jnp.where(lane < back, turned[b], turned[min(b + 1, 2)]).astype(bf16) for b in range(3)
        ]
        for xb in range(2):
            at = v * 320 + xb * 160
            win_ref[at : at + 160, 0:128] = tiles[xb]
            win_ref[at : at + 160, 128:256] = tiles[xb + 1]

    col = lax.broadcasted_iota(jnp.int32, (SIDE, COLS), 1).astype(f32)
    tx = (2.0 * col + 1.0) / COLS - 1.0
    out = []

    def spread(group):
        at = group[0] * 320
        got = jnp.dot(
            win_ref[at : at + 320 * len(group), :], across_ref[...], preferred_element_type=f32
        ).astype(bf16)
        for n, v in enumerate(group):
            stack_ref[v, 960:LONG, :] = jnp.zeros((LONG - 960, COLS), bf16)
            for xb in range(2):
                row = n * 320 + xb * 160
                for i in range(ORDERS):
                    piece = got[row : row + 160, i * 128 : (i + 1) * 128]
                    low = ORDERS * 128 + i * half
                    cols = slice(xb * 128, (xb + 1) * 128)
                    stack_ref[v, i * 128 : (i + 1) * 128, cols] = piece[0:128]
                    stack_ref[v, low : low + half, cols] = piece[128:160]

    def differ(v):
        down = down_ref[v] if v < 3 else far_ref[v - 3]
        parts = jnp.dot(down, stack_ref[v], preferred_element_type=f32)
        model = parts[0:128] + tx * (parts[128:256] + tx * parts[256:384])
        diff_ref[v] = (sci_ref[v].astype(f32) - model).astype(bf16)

    def columns(v):
        filt = jnp.dot(diff_ref[v], colf_ref[v], preferred_element_type=f32).astype(bf16)
        filt_ref[v] = filt
        top_ref[v] = filt[0:HALO]
        bot_ref[v] = filt[SIDE - HALO :]

    def send(group, k, src, dst):
        copy = pltpu.make_async_copy(
            src.at[group[0] : group[-1] + 1], dst.at[group[0] : group[-1] + 1], out_sem.at[k]
        )
        copy.start()
        out.append(copy)

    early, rest = (0, 1, 2), (3, 4, 5)
    for v in early:
        window(v)
    whole[0].wait()
    spread(early)
    for v in rest:
        window(v)
    spread(rest)
    for copy in whole[1:3]:
        copy.wait()
    for v in early:
        differ(v)
    for v in early:
        columns(v)
    whole[3].wait()
    send(early, 0, diff_ref, diff_any)
    send(early, 1, filt_ref, filt_any)
    for v in rest:
        differ(v)
    send(rest, 2, diff_ref, diff_any)
    for v in rest:
        columns(v)
    send(rest, 3, filt_ref, filt_any)
    for copy in out:
        copy.wait()


def score_kernel(filt_any, rowf_any, score_any, part_ref, filt_ref, rowf_ref, score_ref, sem):
    fetch = [
        pltpu.make_async_copy(filt_any, filt_ref, sem.at[0]),
        pltpu.make_async_copy(rowf_any, rowf_ref, sem.at[1]),
    ]
    for copy in fetch:
        copy.start()
    for copy in fetch:
        copy.wait()
    for v in range(VISITS):
        score = jnp.dot(rowf_ref[v, :, 0:128], filt_ref[v], preferred_element_type=f32)
        score_ref[v] = score
        part_ref[v, 0:HALO] = score[0:HALO]
        part_ref[v, HALO:] = score[SIDE - HALO :]
    out = pltpu.make_async_copy(score_ref, score_any, sem.at[2])
    out.start()
    out.wait()


def edge_kernel(part_ref, above_ref, below_ref, rowf_ref, _, score_ref, buf_ref, sem):
    for v in range(VISITS):
        gap = jnp.zeros((128 - 2 * HALO, COLS), bf16)
        ring = jnp.concatenate([below_ref[v], gap, above_ref[v]], axis=0)
        band = jnp.concatenate(
            [rowf_ref[v, 0:HALO, 128:256], rowf_ref[v, SIDE - HALO :, 128:256]], axis=0
        )
        buf_ref[v] = part_ref[v] + jnp.dot(band, ring, preferred_element_type=f32)
    top = pltpu.make_async_copy(buf_ref.at[:, 0:HALO], score_ref.at[:, 0:HALO], sem.at[0])
    bot = pltpu.make_async_copy(
        buf_ref.at[:, HALO : 2 * HALO], score_ref.at[:, SIDE - HALO : SIDE], sem.at[1]
    )
    top.start()
    bot.start()
    top.wait()
    bot.wait()


def sds(shape, dtype):
    return jax.ShapeDtypeStruct(shape, dtype)


def near(x):
    return pltpu.with_memory_space_constraint(x, pltpu.VMEM)


def body(
    science, templates, cell_owner, cell_index, row_offset, col_offset, coefficients, psf_taps
):
    oy = row_offset[:, 0]
    ox = col_offset[:, 0]
    me = lax.axis_index("sky").astype(jnp.int32).reshape(1)

    packed = pl.pallas_call(
        pack_kernel,
        out_shape=pltpu.VMEM((GROUP // 2, 2, PACKED, 128), bf16),
        in_specs=[HB] * 5,
        out_specs=VM,
        scratch_shapes=[
            pltpu.VMEM((CELLS, SIDE, 128), bf16),
            pltpu.VMEM((1, 36), jnp.int32),
            pltpu.VMEM((1, 36), jnp.int32),
            pltpu.VMEM((1, VISITS), jnp.int32),
            pltpu.VMEM((1, VISITS), jnp.int32),
            pltpu.VMEM((8, 128), f32),
            pltpu.SemaphoreType.DMA((5,)),
        ],
        name="pack",
    )(templates, cell_owner.reshape(1, 36), cell_index, oy.reshape(1, 6), ox.reshape(1, 6))
    stripes = lax.all_to_all(packed.reshape(GROUP, PACKED, 128), "sky", 0, 0, tiled=True)

    taps = hermite_table()
    ahead = np.zeros((8, FAR), np.float32)
    ahead[:ORDERS, :TAPS] = taps
    psf = psf_taps.astype(f32)
    zero = jnp.zeros((VISITS, FAR - TAPS), f32)
    colrow = jnp.concatenate([jnp.flip(psf[:, 1], axis=1), zero], axis=1)
    rowrow = jnp.concatenate([psf[:, 0], zero], axis=1)
    psf_rows = jnp.stack([jnp.roll(colrow, -RAD, axis=1), jnp.roll(rowrow, -RAD, axis=1)], axis=1)

    down, far, colf, rowf = pl.pallas_call(
        bands_kernel,
        grid=(VISITS,),
        in_specs=[
            SM, SM,
            pl.BlockSpec((8, FAR), lambda v: (0, 0)),
            pl.BlockSpec((1, 2, FAR), lambda v: (v, 0, 0)),
        ],
        out_specs=[
            VM,
            pl.BlockSpec((1, 384, LONG), lambda v: (jnp.maximum(v - 3, 0), 0, 0)),
            pl.BlockSpec((1, COLS, COLS), lambda v: (v, 0, 0)),
            pl.BlockSpec((1, SIDE, FAR), lambda v: (v, 0, 0)),
        ],
        out_shape=[
            pltpu.VMEM((3, 384, LONG), bf16),
            sds((3, 384, LONG), bf16),
            sds((VISITS, COLS, COLS), bf16),
            sds((VISITS, SIDE, FAR), bf16),
        ],
        scratch_shapes=[
            pltpu.VMEM((384, LONG), bf16),
            pltpu.VMEM((ORDERS, SIDE, FAR), f32),
            pltpu.VMEM((ORDERS, SIDE, FAR), f32),
        ],
        name="bands",
    )(oy, coefficients.reshape(VISITS, 126), jnp.asarray(ahead), psf_rows)
    stripes, colf = lax.optimization_barrier((stripes, colf))

    picked = pl.pallas_call(
        select_kernel,
        out_shape=sds((GROUP, PICKS, 128), bf16),
        in_specs=[SM, VM],
        out_specs=VM,
        scratch_shapes=[pltpu.VMEM((8, GROUP, 128), f32)],
        compiler_params=LIMIT,
        name="select",
    )(me, near(stripes))
    rows = lax.all_to_all(picked, "sky", 0, 0, tiled=True)

    difference, filtered, top, bot = pl.pallas_call(
        model_kernel,
        in_specs=[SM, VM, VM] + [HB] * 4,
        out_specs=[HB, HB, VM, VM],
        out_shape=[
            sds((VISITS, SIDE, COLS), bf16),
            sds((VISITS, SIDE, COLS), bf16),
            sds((VISITS, HALO, COLS), bf16),
            sds((VISITS, HALO, COLS), bf16),
        ],
        scratch_shapes=[
            pltpu.VMEM((FAR, 768), bf16),
            pltpu.VMEM((3, 384, LONG), bf16),
            pltpu.VMEM((VISITS, COLS, COLS), bf16),
            pltpu.VMEM((VISITS, SIDE, COLS), bf16),
            pltpu.VMEM((VISITS, SIDE, COLS), bf16),
            pltpu.VMEM((VISITS, SIDE, COLS), bf16),
            pltpu.VMEM((VISITS * 320, 256), bf16),
            pltpu.VMEM((VISITS, LONG, COLS), bf16),
            pltpu.SemaphoreType.DMA((4,)),
            pltpu.SemaphoreType.DMA((4,)),
        ],
        name="model",
    )(ox, near(rows), near(down), jnp.asarray(across_band(taps)).astype(bf16), far, colf, science)

    count = lax.axis_size("ccd")
    above = lax.ppermute(bot, "ccd", [(i, i + 1) for i in range(count - 1)])
    below = lax.ppermute(top, "ccd", [(i + 1, i) for i in range(count - 1)])

    score, part = pl.pallas_call(
        score_kernel,
        in_specs=[HB, HB],
        out_specs=[HB, VM],
        out_shape=[
            sds((VISITS, SIDE, COLS), f32),
            pltpu.VMEM((VISITS, 2 * HALO, COLS), f32),
        ],
        scratch_shapes=[
            pltpu.VMEM((VISITS, SIDE, COLS), bf16),
            pltpu.VMEM((VISITS, SIDE, FAR), bf16),
            pltpu.VMEM((VISITS, SIDE, COLS), f32),
            pltpu.SemaphoreType.DMA((3,)),
        ],
        name="score",
    )(filtered, rowf)

    score = pl.pallas_call(
        edge_kernel,
        out_shape=sds((VISITS, SIDE, COLS), f32),
        in_specs=[VM, VM, VM, VM, pl.BlockSpec(memory_space=pl.ANY)],
        out_specs=pl.BlockSpec(memory_space=pl.ANY),
        scratch_shapes=[pltpu.VMEM((VISITS, 2 * HALO, COLS), f32), pltpu.SemaphoreType.DMA((2,))],
        input_output_aliases={4: 0},
        compiler_params=LIMIT,
        name="edges",
    )(part, near(above), near(below), rowf, score)
    return difference, score


def solution(mesh):
    in_specs = (
        P("sky", "ccd", None),
        P("sky", "ccd", None),
        P("sky", "ccd", None),
        P("sky", "ccd"),
        P("sky", "ccd"),
        P("sky", "ccd"),
        P("sky", "ccd", None, None),
        P("sky", None, None),
    )
    out_specs = (P("sky", "ccd", None), P("sky", "ccd", None))
    return jax.shard_map(body, mesh=mesh, in_specs=in_specs, out_specs=out_specs, check_vma=False)
```

```python
import jax
import jax.numpy as jnp
import numpy as np
from jax import lax
from jax.experimental import pallas as pl
from jax.experimental.pallas import tpu as pltpu
from jax.sharding import PartitionSpec as P

RAD = 15
TAPS = 31
ORDERS = 6
GROUP = 64
CELLS = 16
SIDE = 128
VISITS = 6
COLS = 256
HALO = 16
STRIPE = 32
PACKED = 40
PICKS = 40
LONG = 1024
MAXOFF = 98
FAR = 256
f32 = jnp.float32
bf16 = jnp.bfloat16
VM = pl.BlockSpec(memory_space=pltpu.VMEM)
HB = pl.BlockSpec(memory_space=pltpu.HBM)
SM = pl.BlockSpec(memory_space=pltpu.SMEM)
LIMIT = pltpu.CompilerParams(vmem_limit_bytes=32 * 2**20)


def hermite_table():
    t = (np.arange(TAPS, dtype=np.float32) - np.float32(RAD)) / np.float32(4.0)
    series = [np.ones(t.shape, np.float32), np.float32(2.0) * t]
    for n in range(1, ORDERS - 1):
        series.append(np.float32(2.0) * t * series[n] - np.float32(2.0 * n) * series[n - 1])
    w = np.stack(series) * np.exp(np.float32(-0.5) * t * t)
    w = w / np.sqrt(np.sum(w * w, axis=1, keepdims=True))
    return np.asarray(w, dtype=jnp.bfloat16).astype(np.float32)


def quarter(x, k):
    return pltpu.roll(x, (k % 4) * 32, 1) if k % 4 else x


def choose(quarters, *items):
    out = items[-1]
    for mask, item in zip(quarters, items[:-1]):
        out = jnp.where(mask, item, out)
    return out


def quarter_masks(count):
    at = lax.broadcasted_iota(jnp.int32, (count, 128), 1) // 32
    return [at == k for k in range(3)]


def transpose_quarters(items, masks):
    turned = [quarter(x, j) for j, x in enumerate(items)]
    return [
        quarter(choose(masks, *(turned[(m - t) % 4] for m in range(4))), -t) for t in range(4)
    ]


def across_band(taps):
    band = np.zeros((FAR, ORDERS * 128), np.float32)
    for i in range(ORDERS):
        for x in range(128):
            band[x : x + TAPS, i * 128 + x] = taps[i]
    return band


def scatter_rows():
    r = lax.broadcasted_iota(jnp.int32, (256, 256), 0)
    c = lax.broadcasted_iota(jnp.int32, (256, 256), 1)
    return jnp.where(c == (r % 8) * 32 + r // 8, 1.0, 0.0).astype(bf16)


def gather_rows():
    r = lax.broadcasted_iota(jnp.int32, (256, 256), 0)
    c = lax.broadcasted_iota(jnp.int32, (256, 256), 1)
    source = ((r % 16) * 2 + (r // 16) % 2) * 8 + r // 32
    return jnp.where(c == source, 1.0, 0.0).astype(bf16)


def pack_kernel(
    cells_any, owner_any, index_any, oy_any, ox_any, out_any,
    cells_ref, owner_ref, index_ref, oy_ref, ox_ref, info_ref, out_ref, sem, out_sem,
):
    cells = [
        pltpu.make_async_copy(
            cells_any.at[h * 8 : (h + 1) * 8], cells_ref.at[h * 8 : (h + 1) * 8], sem.at[h]
        )
        for h in range(2)
    ]
    small = [
        pltpu.make_async_copy(src, dst, sem.at[2 + k])
        for k, (src, dst) in enumerate(
            ((owner_any, owner_ref), (index_any, index_ref), (oy_any, oy_ref), (ox_any, ox_ref))
        )
    ]
    for copy in cells + small:
        copy.start()
    move = scatter_rows()
    masks = quarter_masks(256)
    info_ref[...] = jnp.zeros((8, 128), f32)
    for copy in small:
        copy.wait()
    info_ref[0:1, 0:36] = owner_ref[...].astype(f32)
    info_ref[1:2, 0:36] = index_ref[...].astype(f32)
    info_ref[2:3, 0:VISITS] = oy_ref[...].astype(f32)
    info_ref[3:4, 0:VISITS] = ox_ref[...].astype(f32)
    info = info_ref[...].astype(bf16)
    for d in range(GROUP):
        out_ref[d // 2, d % 2, STRIPE:PACKED, :] = info
    out = []

    def send(at):
        copy = pltpu.make_async_copy(
            out_ref.at[:, :, at : at + 8], out_any.at[:, :, at : at + 8], out_sem.at[at // 8]
        )
        copy.start()
        out.append(copy)

    send(STRIPE)
    for h in range(2):
        cells[h].wait()
        moved = [
            jnp.dot(
                move,
                cells_ref[h * 8 : (h + 1) * 8, q * 32 : (q + 1) * 32, :].reshape(256, 128),
                preferred_element_type=f32,
            )
            for q in range(4)
        ]
        groups = transpose_quarters(moved, masks)
        for u in range(2):
            at = u * CELLS + h * 8
            for c in range(2):
                out_ref[:, c, at : at + 8, :] = groups[c + 2 * u].reshape(32, 8, 128).astype(bf16)
            send(at)
    for copy in out:
        copy.wait()


def select_kernel(me_ref, stripes_ref, out_ref, asks_ref):
    table = jnp.concatenate(
        [
            stripes_ref[:, 0:CELLS, :].reshape(GROUP * CELLS, 128),
            stripes_ref[:, CELLS:STRIPE, :].reshape(GROUP * CELLS, 128),
        ],
        axis=1,
    )
    me = me_ref[0]
    own = (me // 2).astype(f32)
    core = (me % 2).astype(f32)
    for n in range(GROUP):
        asks_ref[:, n, :] = stripes_ref[n, STRIPE:PACKED, :].astype(f32)
    ids = asks_ref[0] * CELLS + asks_ref[1]
    tops = asks_ref[2]
    lefts = asks_ref[3]
    lane = lax.broadcasted_iota(jnp.int32, (GROUP, 128), 1)
    number = [(lane + 128 * k).astype(f32) for k in range(GROUP * CELLS // 128)]
    first = (lane // 32 * 32).astype(f32) + own
    masks = quarter_masks(GROUP)
    move = scatter_rows()

    def column(x, k):
        return jnp.broadcast_to(x[:, k : k + 1], (GROUP, 128))

    lines, last = [], []
    fifths = []
    for v in range(VISITS):
        hot = []
        for r in range(6):
            want = column(ids, v * 6 + r)
            hot.append(
                jnp.concatenate(
                    [jnp.where(n == want, 1.0, 0.0).astype(bf16) for n in number], axis=1
                )
            )
        got = jnp.dot(jnp.concatenate(hot, axis=0), table, preferred_element_type=f32)
        above = first >= column(tops, v)
        late = column(lefts, v) >= 32.0 * (core + 1.0)
        whole, fifth = [], []
        for b in range(3):
            for u in range(2):
                upper = got[b * GROUP : (b + 1) * GROUP, u * 128 : (u + 1) * 128]
                lower = got[(3 + b) * GROUP : (4 + b) * GROUP, u * 128 : (u + 1) * 128]
                whole.append(jnp.where(above, upper, quarter(lower, -1)))
                fifth.append(lower)
        whole[0] = jnp.where(late, whole[5], whole[0])
        fifth[0] = jnp.where(late, fifth[5], fifth[0])
        lines += [w.astype(bf16) for w in whole[:5]]
        fifths.append(choose(masks, *(quarter(fifth[k], k) for k in range(4))).astype(bf16))
        last.append(quarter(fifth[4], v))
    lines += fifths
    lines.append(choose(masks, *last[:4]).astype(bf16))
    lines.append(choose(masks, last[4], last[5], last[5], last[5]).astype(bf16))
    lines += [lines[-1], lines[-1]]
    for k in range(PICKS // 8):
        block = jnp.concatenate(
            [
                jnp.concatenate([x[h * 32 : (h + 1) * 32] for x in lines[k * 8 : k * 8 + 8]], axis=0)
                for h in range(2)
            ],
            axis=1,
        )
        moved = jnp.dot(move, block, preferred_element_type=f32)
        for h in range(2):
            out_ref[h * 32 : (h + 1) * 32, k * 8 : k * 8 + 8, :] = (
                moved[:, h * 128 : (h + 1) * 128].reshape(32, 8, 128).astype(bf16)
            )


def bands_kernel(
    oy_ref, coef_ref, taps_ref, psf_ref,
    near_ref, far_ref, colf_ref, rowf_ref, down_ref, toep_ref, shift_ref,
):
    v = pl.program_id(0)

    def spread(row, count):
        return pltpu.roll(jnp.broadcast_to(row, (count, FAR)), 0, 1, stride=1, stride_axis=0)

    @pl.when(v == 0)
    def _():
        for i in range(ORDERS):
            toep_ref[i] = spread(taps_ref[i : i + 1, :], SIDE)

    oy = oy_ref[v]
    for i in range(ORDERS):
        shift_ref[i] = pltpu.roll(toep_ref[i], oy, 1)
    near = lax.broadcasted_iota(jnp.int32, (COLS, COLS), 0) - lax.broadcasted_iota(
        jnp.int32, (COLS, COLS), 1
    )
    colf_ref[0] = jnp.where(
        jnp.abs(near) <= RAD, spread(psf_ref[0, 0:1, :], COLS), 0.0
    ).astype(bf16)
    rowf_ref[0] = spread(psf_ref[0, 1:2, :], SIDE).astype(bf16)

    masks = quarter_masks(16)
    three = lax.broadcasted_iota(jnp.int32, (16, 128), 1) < 96

    def step(g, _):
        row = lax.broadcasted_iota(jnp.int32, (16, 128), 0) + g * 16
        ty = (2.0 * row.astype(f32) + 1.0) / SIDE - 1.0
        bands = [shift_ref[j, pl.ds(g * 16, 16), :] for j in range(ORDERS)]
        first = 0
        fifth = []
        for i in range(ORDERS):
            sums = [None] * 6
            for j in range(ORDERS - i):
                c = [coef_ref[v, (first + j) * 6 + p] for p in range(6)]
                flat = c[0] + ty * (c[2] + ty * c[5])
                slope = c[1] + ty * c[4]
                for part in range(2):
                    band = bands[j][:, part * 128 : (part + 1) * 128]
                    for q, weight in enumerate((flat, slope, c[3])):
                        term = weight * band
                        at = q * 2 + part
                        sums[at] = term if sums[at] is None else sums[at] + term
            first += ORDERS - i
            ends = []
            for q in range(3):
                low, high = sums[q * 2], sums[q * 2 + 1]
                down_ref[pl.ds(q * SIDE + g * 16, 16), i * 128 : (i + 1) * 128] = (
                    low + jnp.where(three, quarter(high, -1), 0.0)
                ).astype(bf16)
                ends.append(quarter(high, i))
            fifth.append(ends)
        for q in range(3):
            row_at = pl.ds(q * SIDE + g * 16, 16)
            down_ref[row_at, 768:896] = choose(masks, *(fifth[i][q] for i in range(4))).astype(
                bf16
            )
            gap = jnp.zeros((16, 128), f32)
            down_ref[row_at, 896:1024] = choose(
                masks, fifth[4][q], fifth[5][q], gap, gap
            ).astype(bf16)
        return 0

    lax.fori_loop(0, SIDE // 16, step, 0)

    @pl.when(v < 3)
    def _():
        near_ref[0] = down_ref[...]

    @pl.when(v >= 3)
    def _():
        far_ref[0] = down_ref[...]


def model_kernel(
    ox_ref, rows_ref, down_ref, across_any, far_any, colf_any, sci_any,
    diff_ref, filt_ref, top_ref, bot_ref,
    across_ref, far_ref, colf_ref, sci_ref, win_ref, stack_ref, sem,
):
    whole = [
        pltpu.make_async_copy(src, dst, sem.at[k])
        for k, (src, dst) in enumerate(
            (
                (across_any, across_ref), (colf_any, colf_ref), (sci_any, sci_ref),
                (far_any, far_ref),
            )
        )
    ]
    for copy in whole[:3]:
        copy.start()
    half = GROUP // 2
    move = gather_rows()
    masks = quarter_masks(half)
    lane = lax.broadcasted_iota(jnp.int32, (160, 128), 1)
    lines = []
    for k in range(PICKS // 8):
        block = jnp.concatenate(
            [
                rows_ref[h * 32 : (h + 1) * 32, k * 8 : k * 8 + 8, :].reshape(256, 128)
                for h in range(2)
            ],
            axis=1,
        )
        lines.append(jnp.dot(move, block, preferred_element_type=f32))

    def take(row, c):
        at = (row % 8) * 32 + c * 16
        return jnp.concatenate(
            [lines[row // 8][at : at + 16, h * 128 : (h + 1) * 128] for h in range(2)], axis=0
        )

    def window(v):
        groups = [[take(v * 5 + k, c) for c in range(2)] for k in range(5)]
        blocks = [
            transpose_quarters(
                [groups[k][0], groups[k][1], groups[m][0], groups[m][1]], masks
            )
            for k, m in ((0, 1), (2, 3), (4, 0))
        ]
        e = [take(30 + v, c) for c in range(2)]
        f = [take(36 + v // 4, c) for c in range(2)]
        fifths = [
            choose(masks, e[0], quarter(e[1], 1), quarter(e[0], 1), quarter(e[1], 2)),
            choose(masks, quarter(e[0], 2), quarter(e[1], 3), quarter(e[0], 3), e[1]),
            choose(
                masks, quarter(f[0], -v), quarter(f[1], 1 - v), quarter(e[0], 2), quarter(e[1], 3)
            ),
        ]
        back = 128 - ox_ref[v]
        turned = [
            pltpu.roll(jnp.concatenate(blocks[b] + [fifths[b]], axis=0), back, 1)
            for b in range(3)
        ]
        tiles = [
            jnp.where(lane < back, turned[b], turned[min(b + 1, 2)]).astype(bf16) for b in range(3)
        ]
        for xb in range(2):
            at = v * 320 + xb * 160
            win_ref[at : at + 160, 0:128] = tiles[xb]
            win_ref[at : at + 160, 128:256] = tiles[xb + 1]

    col = lax.broadcasted_iota(jnp.int32, (SIDE, COLS), 1).astype(f32)
    tx = (2.0 * col + 1.0) / COLS - 1.0

    def spread(group):
        at = group[0] * 320
        got = jnp.dot(
            win_ref[at : at + 320 * len(group), :], across_ref[...], preferred_element_type=f32
        ).astype(bf16)
        for n, v in enumerate(group):
            stack_ref[v, 960:LONG, :] = jnp.zeros((LONG - 960, COLS), bf16)
            for xb in range(2):
                row = n * 320 + xb * 160
                for i in range(ORDERS):
                    piece = got[row : row + 160, i * 128 : (i + 1) * 128]
                    low = ORDERS * 128 + i * half
                    cols = slice(xb * 128, (xb + 1) * 128)
                    stack_ref[v, i * 128 : (i + 1) * 128, cols] = piece[0:128]
                    stack_ref[v, low : low + half, cols] = piece[128:160]

    def differ(v):
        down = down_ref[v] if v < 3 else far_ref[v - 3]
        parts = jnp.dot(down, stack_ref[v], preferred_element_type=f32)
        model = parts[0:128] + tx * (parts[128:256] + tx * parts[256:384])
        diff_ref[v] = (sci_ref[v].astype(f32) - model).astype(bf16)

    def columns(v):
        filt = jnp.dot(diff_ref[v], colf_ref[v], preferred_element_type=f32).astype(bf16)
        filt_ref[v] = filt
        top_ref[v] = filt[0:HALO]
        bot_ref[v] = filt[SIDE - HALO :]

    early, rest = (0, 1, 2), (3, 4, 5)
    for v in early:
        window(v)
    whole[0].wait()
    whole[3].start()
    spread(early)
    for v in rest:
        window(v)
    spread(rest)
    for copy in whole[1:3]:
        copy.wait()
    for v in early:
        differ(v)
    for v in early:
        columns(v)
    whole[3].wait()
    for v in rest:
        differ(v)
    for v in rest:
        columns(v)


def score_kernel(filt_ref, diff_ref, rowf_any, diff_any, score_any, part_ref, rowf_ref, score_ref, sem):
    rows = pltpu.make_async_copy(rowf_any, rowf_ref, sem.at[0])
    keep = pltpu.make_async_copy(diff_ref, diff_any, sem.at[1])
    rows.start()
    keep.start()
    rows.wait()
    for v in range(VISITS):
        score = jnp.dot(rowf_ref[v, :, 0:128], filt_ref[v], preferred_element_type=f32)
        score_ref[v] = score
        part_ref[v, 0:HALO] = score[0:HALO]
        part_ref[v, HALO:] = score[SIDE - HALO :]
    done = pltpu.make_async_copy(score_ref, score_any, sem.at[2])
    done.start()
    keep.wait()
    done.wait()


def edge_kernel(part_ref, above_ref, below_ref, rowf_ref, _, score_ref, buf_ref, sem):
    for v in range(VISITS):
        gap = jnp.zeros((128 - 2 * HALO, COLS), bf16)
        ring = jnp.concatenate([below_ref[v], gap, above_ref[v]], axis=0)
        band = jnp.concatenate(
            [rowf_ref[v, 0:HALO, 128:256], rowf_ref[v, SIDE - HALO :, 128:256]], axis=0
        )
        buf_ref[v] = part_ref[v] + jnp.dot(band, ring, preferred_element_type=f32)
    top = pltpu.make_async_copy(buf_ref.at[:, 0:HALO], score_ref.at[:, 0:HALO], sem.at[0])
    bot = pltpu.make_async_copy(
        buf_ref.at[:, HALO : 2 * HALO], score_ref.at[:, SIDE - HALO : SIDE], sem.at[1]
    )
    top.start()
    bot.start()
    top.wait()
    bot.wait()


def sds(shape, dtype):
    return jax.ShapeDtypeStruct(shape, dtype)


def near(x):
    return pltpu.with_memory_space_constraint(x, pltpu.VMEM)


def body(
    science, templates, cell_owner, cell_index, row_offset, col_offset, coefficients, psf_taps
):
    oy = row_offset[:, 0]
    ox = col_offset[:, 0]
    me = lax.axis_index("sky").astype(jnp.int32).reshape(1)

    packed = pl.pallas_call(
        pack_kernel,
        out_shape=sds((GROUP // 2, 2, PACKED, 128), bf16),
        in_specs=[HB] * 5,
        out_specs=HB,
        scratch_shapes=[
            pltpu.VMEM((CELLS, SIDE, 128), bf16),
            pltpu.VMEM((1, 36), jnp.int32),
            pltpu.VMEM((1, 36), jnp.int32),
            pltpu.VMEM((1, VISITS), jnp.int32),
            pltpu.VMEM((1, VISITS), jnp.int32),
            pltpu.VMEM((8, 128), f32),
            pltpu.VMEM((GROUP // 2, 2, PACKED, 128), bf16),
            pltpu.SemaphoreType.DMA((6,)),
            pltpu.SemaphoreType.DMA((5,)),
        ],
        name="pack",
    )(templates, cell_owner.reshape(1, 36), cell_index, oy.reshape(1, 6), ox.reshape(1, 6))
    stripes = lax.all_to_all(packed.reshape(GROUP, PACKED, 128), "sky", 0, 0, tiled=True)

    taps = hermite_table()
    ahead = np.zeros((8, FAR), np.float32)
    ahead[:ORDERS, :TAPS] = taps
    psf = psf_taps.astype(f32)
    zero = jnp.zeros((VISITS, FAR - TAPS), f32)
    colrow = jnp.concatenate([jnp.flip(psf[:, 1], axis=1), zero], axis=1)
    rowrow = jnp.concatenate([psf[:, 0], zero], axis=1)
    psf_rows = jnp.stack([jnp.roll(colrow, -RAD, axis=1), jnp.roll(rowrow, -RAD, axis=1)], axis=1)

    down, far, colf, rowf = pl.pallas_call(
        bands_kernel,
        grid=(VISITS,),
        in_specs=[
            SM, SM,
            pl.BlockSpec((8, FAR), lambda v: (0, 0)),
            pl.BlockSpec((1, 2, FAR), lambda v: (v, 0, 0)),
        ],
        out_specs=[
            pl.BlockSpec((1, 384, LONG), lambda v: (jnp.minimum(v, 2), 0, 0)),
            pl.BlockSpec((1, 384, LONG), lambda v: (jnp.maximum(v - 3, 0), 0, 0)),
            pl.BlockSpec((1, COLS, COLS), lambda v: (v, 0, 0)),
            pl.BlockSpec((1, SIDE, FAR), lambda v: (v, 0, 0)),
        ],
        out_shape=[
            sds((3, 384, LONG), bf16),
            sds((3, 384, LONG), bf16),
            sds((VISITS, COLS, COLS), bf16),
            sds((VISITS, SIDE, FAR), bf16),
        ],
        scratch_shapes=[
            pltpu.VMEM((384, LONG), bf16),
            pltpu.VMEM((ORDERS, SIDE, FAR), f32),
            pltpu.VMEM((ORDERS, SIDE, FAR), f32),
        ],
        name="bands",
    )(oy, coefficients.reshape(VISITS, 126), jnp.asarray(ahead), psf_rows)
    stripes, colf = lax.optimization_barrier((stripes, colf))

    picked = pl.pallas_call(
        select_kernel,
        out_shape=sds((GROUP, PICKS, 128), bf16),
        in_specs=[SM, VM],
        out_specs=VM,
        scratch_shapes=[pltpu.VMEM((8, GROUP, 128), f32)],
        compiler_params=LIMIT,
        name="select",
    )(me, near(stripes))
    rows = lax.all_to_all(picked, "sky", 0, 0, tiled=True)

    near_diff, filtered, top, bot = pl.pallas_call(
        model_kernel,
        in_specs=[SM, VM, VM] + [HB] * 4,
        out_specs=[VM] * 4,
        out_shape=[
            pltpu.VMEM((VISITS, SIDE, COLS), bf16),
            pltpu.VMEM((VISITS, SIDE, COLS), bf16),
            sds((VISITS, HALO, COLS), bf16),
            sds((VISITS, HALO, COLS), bf16),
        ],
        scratch_shapes=[
            pltpu.VMEM((FAR, 768), bf16),
            pltpu.VMEM((3, 384, LONG), bf16),
            pltpu.VMEM((VISITS, COLS, COLS), bf16),
            pltpu.VMEM((VISITS, SIDE, COLS), bf16),
            pltpu.VMEM((VISITS * 320, 256), bf16),
            pltpu.VMEM((VISITS, LONG, COLS), bf16),
            pltpu.SemaphoreType.DMA((4,)),
        ],
        compiler_params=pltpu.CompilerParams(vmem_limit_bytes=61600 * 1024),
        name="model",
    )(ox, near(rows), near(down), jnp.asarray(across_band(taps)).astype(bf16), far, colf, science)

    count = lax.axis_size("ccd")
    above = lax.ppermute(bot, "ccd", [(i, i + 1) for i in range(count - 1)])
    below = lax.ppermute(top, "ccd", [(i + 1, i) for i in range(count - 1)])

    difference, score, part = pl.pallas_call(
        score_kernel,
        in_specs=[VM, VM, HB],
        out_specs=[HB, HB, VM],
        out_shape=[
            sds((VISITS, SIDE, COLS), bf16),
            sds((VISITS, SIDE, COLS), f32),
            pltpu.VMEM((VISITS, 2 * HALO, COLS), f32),
        ],
        scratch_shapes=[
            pltpu.VMEM((VISITS, SIDE, FAR), bf16),
            pltpu.VMEM((VISITS, SIDE, COLS), f32),
            pltpu.SemaphoreType.DMA((3,)),
        ],
        compiler_params=LIMIT,
        name="score",
    )(near(filtered), near(near_diff), rowf)

    score = pl.pallas_call(
        edge_kernel,
        out_shape=sds((VISITS, SIDE, COLS), f32),
        in_specs=[VM, VM, VM, VM, pl.BlockSpec(memory_space=pl.ANY)],
        out_specs=pl.BlockSpec(memory_space=pl.ANY),
        scratch_shapes=[pltpu.VMEM((VISITS, 2 * HALO, COLS), f32), pltpu.SemaphoreType.DMA((2,))],
        input_output_aliases={4: 0},
        compiler_params=LIMIT,
        name="edges",
    )(part, near(above), near(below), rowf, score)
    return difference, score


def solution(mesh):
    in_specs = (
        P("sky", "ccd", None),
        P("sky", "ccd", None),
        P("sky", "ccd", None),
        P("sky", "ccd"),
        P("sky", "ccd"),
        P("sky", "ccd"),
        P("sky", "ccd", None, None),
        P("sky", None, None),
    )
    out_specs = (P("sky", "ccd", None), P("sky", "ccd", None))
    return jax.shard_map(body, mesh=mesh, in_specs=in_specs, out_specs=out_specs, check_vma=False)
```

```python
import jax
import jax.numpy as jnp
import numpy as np
from jax import lax
from jax.experimental import pallas as pl
from jax.experimental.pallas import tpu as pltpu
from jax.sharding import PartitionSpec as P

RAD = 15
TAPS = 31
ORDERS = 6
GROUP = 64
CELLS = 16
SIDE = 128
VISITS = 6
COLS = 256
HALO = 16
STRIPE = 32
PACKED = 40
PICKS = 40
LONG = 1024
MAXOFF = 98
FAR = 256
f32 = jnp.float32
bf16 = jnp.bfloat16
VM = pl.BlockSpec(memory_space=pltpu.VMEM)
HB = pl.BlockSpec(memory_space=pltpu.HBM)
SM = pl.BlockSpec(memory_space=pltpu.SMEM)
LIMIT = pltpu.CompilerParams(vmem_limit_bytes=32 * 2**20)


def hermite_table():
    t = (np.arange(TAPS, dtype=np.float32) - np.float32(RAD)) / np.float32(4.0)
    series = [np.ones(t.shape, np.float32), np.float32(2.0) * t]
    for n in range(1, ORDERS - 1):
        series.append(np.float32(2.0) * t * series[n] - np.float32(2.0 * n) * series[n - 1])
    w = np.stack(series) * np.exp(np.float32(-0.5) * t * t)
    w = w / np.sqrt(np.sum(w * w, axis=1, keepdims=True))
    return np.asarray(w, dtype=jnp.bfloat16).astype(np.float32)


def quarter(x, k):
    return pltpu.roll(x, (k % 4) * 32, 1) if k % 4 else x


def choose(quarters, *items):
    out = items[-1]
    for mask, item in zip(quarters, items[:-1]):
        out = jnp.where(mask, item, out)
    return out


def quarter_masks(count):
    at = lax.broadcasted_iota(jnp.int32, (count, 128), 1) // 32
    return [at == k for k in range(3)]


def transpose_quarters(items, masks):
    turned = [quarter(x, j) for j, x in enumerate(items)]
    return [
        quarter(choose(masks, *(turned[(m - t) % 4] for m in range(4))), -t) for t in range(4)
    ]


def across_band(taps):
    band = np.zeros((FAR, ORDERS * 128), np.float32)
    for i in range(ORDERS):
        for x in range(128):
            band[x : x + TAPS, i * 128 + x] = taps[i]
    return band


def scatter_rows():
    r = lax.broadcasted_iota(jnp.int32, (256, 256), 0)
    c = lax.broadcasted_iota(jnp.int32, (256, 256), 1)
    return jnp.where(c == (r % 8) * 32 + r // 8, 1.0, 0.0).astype(bf16)


def gather_rows():
    r = lax.broadcasted_iota(jnp.int32, (256, 256), 0)
    c = lax.broadcasted_iota(jnp.int32, (256, 256), 1)
    source = ((r % 16) * 2 + (r // 16) % 2) * 8 + r // 32
    return jnp.where(c == source, 1.0, 0.0).astype(bf16)


def pack_kernel(
    cells_any, owner_any, index_any, oy_any, ox_any, out_ref,
    cells_ref, owner_ref, index_ref, oy_ref, ox_ref, info_ref, sem,
):
    copies = [
        pltpu.make_async_copy(src, dst, sem.at[k])
        for k, (src, dst) in enumerate(
            (
                (cells_any, cells_ref), (owner_any, owner_ref), (index_any, index_ref),
                (oy_any, oy_ref), (ox_any, ox_ref),
            )
        )
    ]
    for copy in copies:
        copy.start()
    move = scatter_rows()
    masks = quarter_masks(256)
    info_ref[...] = jnp.zeros((8, 128), f32)
    for copy in copies[1:]:
        copy.wait()
    info_ref[0:1, 0:36] = owner_ref[...].astype(f32)
    info_ref[1:2, 0:36] = index_ref[...].astype(f32)
    info_ref[2:3, 0:VISITS] = oy_ref[...].astype(f32)
    info_ref[3:4, 0:VISITS] = ox_ref[...].astype(f32)
    info = info_ref[...].astype(bf16)
    for d in range(GROUP):
        out_ref[d // 2, d % 2, STRIPE:PACKED, :] = info
    copies[0].wait()
    moved = []
    for q in range(4):
        halves = [
            cells_ref[h * 8 : (h + 1) * 8, q * 32 : (q + 1) * 32, :].reshape(256, 128)
            for h in range(2)
        ]
        moved.append(
            jnp.dot(move, jnp.concatenate(halves, axis=1), preferred_element_type=f32)
        )
    for h in range(2):
        groups = transpose_quarters([m[:, h * 128 : (h + 1) * 128] for m in moved], masks)
        for c in range(2):
            for u in range(2):
                at = u * CELLS + h * 8
                out_ref[:, c, at : at + 8, :] = groups[c + 2 * u].reshape(32, 8, 128).astype(bf16)


def select_kernel(me_ref, stripes_ref, out_ref, asks_ref):
    table = jnp.concatenate(
        [
            stripes_ref[:, 0:CELLS, :].reshape(GROUP * CELLS, 128),
            stripes_ref[:, CELLS:STRIPE, :].reshape(GROUP * CELLS, 128),
        ],
        axis=1,
    )
    me = me_ref[0]
    own = (me // 2).astype(f32)
    core = (me % 2).astype(f32)
    for n in range(GROUP):
        asks_ref[:, n, :] = stripes_ref[n, STRIPE:PACKED, :].astype(f32)
    ids = asks_ref[0] * CELLS + asks_ref[1]
    tops = asks_ref[2]
    lefts = asks_ref[3]
    lane = lax.broadcasted_iota(jnp.int32, (GROUP, 128), 1)
    number = [(lane + 128 * k).astype(f32) for k in range(GROUP * CELLS // 128)]
    first = (lane // 32 * 32).astype(f32) + own
    masks = quarter_masks(GROUP)
    move = scatter_rows()

    def column(x, k):
        return jnp.broadcast_to(x[:, k : k + 1], (GROUP, 128))

    lines, last = [], []
    fifths = []
    for v in range(VISITS):
        hot = []
        for r in range(6):
            want = column(ids, v * 6 + r)
            hot.append(
                jnp.concatenate(
                    [jnp.where(n == want, 1.0, 0.0).astype(bf16) for n in number], axis=1
                )
            )
        got = jnp.dot(jnp.concatenate(hot, axis=0), table, preferred_element_type=f32)
        above = first >= column(tops, v)
        late = column(lefts, v) >= 32.0 * (core + 1.0)
        whole, fifth = [], []
        for b in range(3):
            for u in range(2):
                upper = got[b * GROUP : (b + 1) * GROUP, u * 128 : (u + 1) * 128]
                lower = got[(3 + b) * GROUP : (4 + b) * GROUP, u * 128 : (u + 1) * 128]
                whole.append(jnp.where(above, upper, quarter(lower, -1)))
                fifth.append(lower)
        whole[0] = jnp.where(late, whole[5], whole[0])
        fifth[0] = jnp.where(late, fifth[5], fifth[0])
        lines += [w.astype(bf16) for w in whole[:5]]
        fifths.append(choose(masks, *(quarter(fifth[k], k) for k in range(4))).astype(bf16))
        last.append(quarter(fifth[4], v))
    lines += fifths
    lines.append(choose(masks, *last[:4]).astype(bf16))
    lines.append(choose(masks, last[4], last[5], last[5], last[5]).astype(bf16))
    lines += [lines[-1], lines[-1]]
    for k in range(PICKS // 8):
        block = jnp.concatenate(
            [
                jnp.concatenate([x[h * 32 : (h + 1) * 32] for x in lines[k * 8 : k * 8 + 8]], axis=0)
                for h in range(2)
            ],
            axis=1,
        )
        moved = jnp.dot(move, block, preferred_element_type=f32)
        for h in range(2):
            out_ref[h * 32 : (h + 1) * 32, k * 8 : k * 8 + 8, :] = (
                moved[:, h * 128 : (h + 1) * 128].reshape(32, 8, 128).astype(bf16)
            )


def bands_kernel(
    oy_ref, coef_ref, taps_ref, psf_ref,
    near_ref, far_ref, colf_ref, rowf_ref, down_ref, toep_ref, shift_ref,
):
    v = pl.program_id(0)

    def spread(row, count):
        return pltpu.roll(jnp.broadcast_to(row, (count, FAR)), 0, 1, stride=1, stride_axis=0)

    @pl.when(v == 0)
    def _():
        for i in range(ORDERS):
            toep_ref[i] = spread(taps_ref[i : i + 1, :], SIDE)

    oy = oy_ref[v]
    for i in range(ORDERS):
        shift_ref[i] = pltpu.roll(toep_ref[i], oy, 1)
    near = lax.broadcasted_iota(jnp.int32, (COLS, COLS), 0) - lax.broadcasted_iota(
        jnp.int32, (COLS, COLS), 1
    )
    colf_ref[0] = jnp.where(
        jnp.abs(near) <= RAD, spread(psf_ref[0, 0:1, :], COLS), 0.0
    ).astype(bf16)
    rowf_ref[0] = spread(psf_ref[0, 1:2, :], SIDE).astype(bf16)

    masks = quarter_masks(16)
    three = lax.broadcasted_iota(jnp.int32, (16, 128), 1) < 96

    def step(g, _):
        row = lax.broadcasted_iota(jnp.int32, (16, 128), 0) + g * 16
        ty = (2.0 * row.astype(f32) + 1.0) / SIDE - 1.0
        bands = [shift_ref[j, pl.ds(g * 16, 16), :] for j in range(ORDERS)]
        first = 0
        fifth = []
        for i in range(ORDERS):
            sums = [None] * 6
            for j in range(ORDERS - i):
                c = [coef_ref[v, (first + j) * 6 + p] for p in range(6)]
                flat = c[0] + ty * (c[2] + ty * c[5])
                slope = c[1] + ty * c[4]
                for part in range(2):
                    band = bands[j][:, part * 128 : (part + 1) * 128]
                    for q, weight in enumerate((flat, slope, c[3])):
                        term = weight * band
                        at = q * 2 + part
                        sums[at] = term if sums[at] is None else sums[at] + term
            first += ORDERS - i
            ends = []
            for q in range(3):
                low, high = sums[q * 2], sums[q * 2 + 1]
                down_ref[pl.ds(q * SIDE + g * 16, 16), i * 128 : (i + 1) * 128] = (
                    low + jnp.where(three, quarter(high, -1), 0.0)
                ).astype(bf16)
                ends.append(quarter(high, i))
            fifth.append(ends)
        for q in range(3):
            row_at = pl.ds(q * SIDE + g * 16, 16)
            down_ref[row_at, 768:896] = choose(masks, *(fifth[i][q] for i in range(4))).astype(
                bf16
            )
            gap = jnp.zeros((16, 128), f32)
            down_ref[row_at, 896:1024] = choose(
                masks, fifth[4][q], fifth[5][q], gap, gap
            ).astype(bf16)
        return 0

    lax.fori_loop(0, SIDE // 16, step, 0)

    @pl.when(v < 3)
    def _():
        near_ref[v] = down_ref[...]

    @pl.when(v >= 3)
    def _():
        far_ref[0] = down_ref[...]


def model_kernel(
    ox_ref, rows_ref, down_ref, across_any, far_any, colf_any, sci_any,
    diff_any, filt_ref, top_ref, bot_ref,
    across_ref, far_ref, colf_ref, sci_ref, diff_ref, win_ref, stack_ref, sem,
):
    whole = [
        pltpu.make_async_copy(src, dst, sem.at[k])
        for k, (src, dst) in enumerate(
            (
                (across_any, across_ref), (colf_any, colf_ref), (sci_any, sci_ref),
                (far_any, far_ref),
            )
        )
    ]
    for copy in whole[:3]:
        copy.start()
    half = GROUP // 2
    move = gather_rows()
    masks = quarter_masks(half)
    lane = lax.broadcasted_iota(jnp.int32, (160, 128), 1)
    lines = []
    for k in range(PICKS // 8):
        block = jnp.concatenate(
            [
                rows_ref[h * 32 : (h + 1) * 32, k * 8 : k * 8 + 8, :].reshape(256, 128)
                for h in range(2)
            ],
            axis=1,
        )
        lines.append(jnp.dot(move, block, preferred_element_type=f32))

    def take(row, c):
        at = (row % 8) * 32 + c * 16
        return jnp.concatenate(
            [lines[row // 8][at : at + 16, h * 128 : (h + 1) * 128] for h in range(2)], axis=0
        )

    def window(v):
        groups = [[take(v * 5 + k, c) for c in range(2)] for k in range(5)]
        blocks = [
            transpose_quarters(
                [groups[k][0], groups[k][1], groups[m][0], groups[m][1]], masks
            )
            for k, m in ((0, 1), (2, 3), (4, 0))
        ]
        e = [take(30 + v, c) for c in range(2)]
        f = [take(36 + v // 4, c) for c in range(2)]
        fifths = [
            choose(masks, e[0], quarter(e[1], 1), quarter(e[0], 1), quarter(e[1], 2)),
            choose(masks, quarter(e[0], 2), quarter(e[1], 3), quarter(e[0], 3), e[1]),
            choose(
                masks, quarter(f[0], -v), quarter(f[1], 1 - v), quarter(e[0], 2), quarter(e[1], 3)
            ),
        ]
        back = 128 - ox_ref[v]
        turned = [
            pltpu.roll(jnp.concatenate(blocks[b] + [fifths[b]], axis=0), back, 1)
            for b in range(3)
        ]
        tiles = [
            jnp.where(lane < back, turned[b], turned[min(b + 1, 2)]).astype(bf16) for b in range(3)
        ]
        for xb in range(2):
            at = v * 320 + xb * 160
            win_ref[at : at + 160, 0:128] = tiles[xb]
            win_ref[at : at + 160, 128:256] = tiles[xb + 1]

    col = lax.broadcasted_iota(jnp.int32, (SIDE, COLS), 1).astype(f32)
    tx = (2.0 * col + 1.0) / COLS - 1.0

    def spread(group):
        at = group[0] * 320
        got = jnp.dot(
            win_ref[at : at + 320 * len(group), :], across_ref[...], preferred_element_type=f32
        ).astype(bf16)
        for n, v in enumerate(group):
            stack_ref[v, 960:LONG, :] = jnp.zeros((LONG - 960, COLS), bf16)
            for xb in range(2):
                row = n * 320 + xb * 160
                for i in range(ORDERS):
                    piece = got[row : row + 160, i * 128 : (i + 1) * 128]
                    low = ORDERS * 128 + i * half
                    cols = slice(xb * 128, (xb + 1) * 128)
                    stack_ref[v, i * 128 : (i + 1) * 128, cols] = piece[0:128]
                    stack_ref[v, low : low + half, cols] = piece[128:160]

    def differ(v):
        down = down_ref[v] if v < 3 else far_ref[v - 3]
        parts = jnp.dot(down, stack_ref[v], preferred_element_type=f32)
        model = parts[0:128] + tx * (parts[128:256] + tx * parts[256:384])
        diff_ref[v] = (sci_ref[v].astype(f32) - model).astype(bf16)

    def columns(v):
        filt = jnp.dot(diff_ref[v], colf_ref[v], preferred_element_type=f32).astype(bf16)
        filt_ref[v] = filt
        top_ref[v] = filt[0:HALO]
        bot_ref[v] = filt[SIDE - HALO :]

    early, rest = (0, 1, 2), (3, 4, 5)
    for v in (0, 1, 2, 3):
        window(v)
    whole[0].wait()
    whole[3].start()
    spread(early)
    for v in (4, 5):
        window(v)
    spread(rest)
    for copy in whole[1:3]:
        copy.wait()
    for v in early:
        differ(v)
    for v in early:
        columns(v)
    whole[3].wait()
    out = [
        pltpu.make_async_copy(diff_ref.at[n : n + 3], diff_any.at[n : n + 3], sem.at[4 + n // 3])
        for n in (0, 3)
    ]
    out[0].start()
    for v in rest:
        differ(v)
    out[1].start()
    for v in rest:
        columns(v)
    for copy in out:
        copy.wait()


def score_kernel(filt_ref, rowf_any, score_any, part_ref, rowf_ref, score_ref, sem):
    rows = pltpu.make_async_copy(rowf_any, rowf_ref, sem.at[0])
    rows.start()
    rows.wait()
    for v in range(VISITS):
        score = jnp.dot(rowf_ref[v, :, 0:128], filt_ref[v], preferred_element_type=f32)
        score_ref[v] = score
        part_ref[v, 0:HALO] = score[0:HALO]
        part_ref[v, HALO:] = score[SIDE - HALO :]
    done = pltpu.make_async_copy(score_ref, score_any, sem.at[1])
    done.start()
    done.wait()


def edge_kernel(part_ref, above_ref, below_ref, rowf_ref, _, score_ref, buf_ref, sem):
    for v in range(VISITS):
        gap = jnp.zeros((128 - 2 * HALO, COLS), bf16)
        ring = jnp.concatenate([below_ref[v], gap, above_ref[v]], axis=0)
        band = jnp.concatenate(
            [rowf_ref[v, 0:HALO, 128:256], rowf_ref[v, SIDE - HALO :, 128:256]], axis=0
        )
        buf_ref[v] = part_ref[v] + jnp.dot(band, ring, preferred_element_type=f32)
    top = pltpu.make_async_copy(buf_ref.at[:, 0:HALO], score_ref.at[:, 0:HALO], sem.at[0])
    bot = pltpu.make_async_copy(
        buf_ref.at[:, HALO : 2 * HALO], score_ref.at[:, SIDE - HALO : SIDE], sem.at[1]
    )
    top.start()
    bot.start()
    top.wait()
    bot.wait()


def sds(shape, dtype):
    return jax.ShapeDtypeStruct(shape, dtype)


def near(x):
    return pltpu.with_memory_space_constraint(x, pltpu.VMEM)


def body(
    science, templates, cell_owner, cell_index, row_offset, col_offset, coefficients, psf_taps
):
    oy = row_offset[:, 0]
    ox = col_offset[:, 0]
    me = lax.axis_index("sky").astype(jnp.int32).reshape(1)

    packed = pl.pallas_call(
        pack_kernel,
        out_shape=pltpu.VMEM((GROUP // 2, 2, PACKED, 128), bf16),
        in_specs=[HB] * 5,
        out_specs=VM,
        scratch_shapes=[
            pltpu.VMEM((CELLS, SIDE, 128), bf16),
            pltpu.VMEM((1, 36), jnp.int32),
            pltpu.VMEM((1, 36), jnp.int32),
            pltpu.VMEM((1, VISITS), jnp.int32),
            pltpu.VMEM((1, VISITS), jnp.int32),
            pltpu.VMEM((8, 128), f32),
            pltpu.SemaphoreType.DMA((5,)),
        ],
        name="pack",
    )(templates, cell_owner.reshape(1, 36), cell_index, oy.reshape(1, 6), ox.reshape(1, 6))
    stripes = lax.all_to_all(packed.reshape(GROUP, PACKED, 128), "sky", 0, 0, tiled=True)

    taps = hermite_table()
    ahead = np.zeros((8, FAR), np.float32)
    ahead[:ORDERS, :TAPS] = taps
    psf = psf_taps.astype(f32)
    zero = jnp.zeros((VISITS, FAR - TAPS), f32)
    colrow = jnp.concatenate([jnp.flip(psf[:, 1], axis=1), zero], axis=1)
    rowrow = jnp.concatenate([psf[:, 0], zero], axis=1)
    psf_rows = jnp.stack([jnp.roll(colrow, -RAD, axis=1), jnp.roll(rowrow, -RAD, axis=1)], axis=1)

    down, far, colf, rowf = pl.pallas_call(
        bands_kernel,
        grid=(VISITS,),
        in_specs=[
            SM, SM,
            pl.BlockSpec((8, FAR), lambda v: (0, 0)),
            pl.BlockSpec((1, 2, FAR), lambda v: (v, 0, 0)),
        ],
        out_specs=[
            VM,
            pl.BlockSpec((1, 384, LONG), lambda v: (jnp.maximum(v - 3, 0), 0, 0)),
            pl.BlockSpec((1, COLS, COLS), lambda v: (v, 0, 0)),
            pl.BlockSpec((1, SIDE, FAR), lambda v: (v, 0, 0)),
        ],
        out_shape=[
            pltpu.VMEM((3, 384, LONG), bf16),
            sds((3, 384, LONG), bf16),
            sds((VISITS, COLS, COLS), bf16),
            sds((VISITS, SIDE, FAR), bf16),
        ],
        scratch_shapes=[
            pltpu.VMEM((384, LONG), bf16),
            pltpu.VMEM((ORDERS, SIDE, FAR), f32),
            pltpu.VMEM((ORDERS, SIDE, FAR), f32),
        ],
        name="bands",
    )(oy, coefficients.reshape(VISITS, 126), jnp.asarray(ahead), psf_rows)
    stripes, colf = lax.optimization_barrier((stripes, colf))

    picked = pl.pallas_call(
        select_kernel,
        out_shape=sds((GROUP, PICKS, 128), bf16),
        in_specs=[SM, VM],
        out_specs=VM,
        scratch_shapes=[pltpu.VMEM((8, GROUP, 128), f32)],
        compiler_params=LIMIT,
        name="select",
    )(me, near(stripes))
    rows = lax.all_to_all(picked, "sky", 0, 0, tiled=True)

    difference, filtered, top, bot = pl.pallas_call(
        model_kernel,
        in_specs=[SM, VM, VM] + [HB] * 4,
        out_specs=[HB, VM, VM, VM],
        out_shape=[
            sds((VISITS, SIDE, COLS), bf16),
            pltpu.VMEM((VISITS, SIDE, COLS), bf16),
            sds((VISITS, HALO, COLS), bf16),
            sds((VISITS, HALO, COLS), bf16),
        ],
        scratch_shapes=[
            pltpu.VMEM((FAR, 768), bf16),
            pltpu.VMEM((3, 384, LONG), bf16),
            pltpu.VMEM((VISITS, COLS, COLS), bf16),
            pltpu.VMEM((VISITS, SIDE, COLS), bf16),
            pltpu.VMEM((VISITS, SIDE, COLS), bf16),
            pltpu.VMEM((VISITS * 320, 256), bf16),
            pltpu.VMEM((VISITS, LONG, COLS), bf16),
            pltpu.SemaphoreType.DMA((6,)),
        ],
        name="model",
    )(ox, near(rows), near(down), jnp.asarray(across_band(taps)).astype(bf16), far, colf, science)

    count = lax.axis_size("ccd")
    above = lax.ppermute(bot, "ccd", [(i, i + 1) for i in range(count - 1)])
    below = lax.ppermute(top, "ccd", [(i + 1, i) for i in range(count - 1)])

    score, part = pl.pallas_call(
        score_kernel,
        in_specs=[VM, HB],
        out_specs=[HB, VM],
        out_shape=[
            sds((VISITS, SIDE, COLS), f32),
            pltpu.VMEM((VISITS, 2 * HALO, COLS), f32),
        ],
        scratch_shapes=[
            pltpu.VMEM((VISITS, SIDE, FAR), bf16),
            pltpu.VMEM((VISITS, SIDE, COLS), f32),
            pltpu.SemaphoreType.DMA((2,)),
        ],
        compiler_params=LIMIT,
        name="score",
    )(near(filtered), rowf)

    score = pl.pallas_call(
        edge_kernel,
        out_shape=sds((VISITS, SIDE, COLS), f32),
        in_specs=[VM, VM, VM, VM, pl.BlockSpec(memory_space=pl.ANY)],
        out_specs=pl.BlockSpec(memory_space=pl.ANY),
        scratch_shapes=[pltpu.VMEM((VISITS, 2 * HALO, COLS), f32), pltpu.SemaphoreType.DMA((2,))],
        input_output_aliases={4: 0},
        compiler_params=LIMIT,
        name="edges",
    )(part, near(above), near(below), rowf, score)
    return difference, score


def solution(mesh):
    in_specs = (
        P("sky", "ccd", None),
        P("sky", "ccd", None),
        P("sky", "ccd", None),
        P("sky", "ccd"),
        P("sky", "ccd"),
        P("sky", "ccd"),
        P("sky", "ccd", None, None),
        P("sky", None, None),
    )
    out_specs = (P("sky", "ccd", None), P("sky", "ccd", None))
    return jax.shard_map(body, mesh=mesh, in_specs=in_specs, out_specs=out_specs, check_vma=False)
```

```python
import jax
import jax.numpy as jnp
import numpy as np
from jax import lax
from jax.experimental import pallas as pl
from jax.experimental.pallas import tpu as pltpu
from jax.sharding import PartitionSpec as P

RAD = 15
TAPS = 31
ORDERS = 6
GROUP = 64
CELLS = 16
SIDE = 128
VISITS = 6
COLS = 256
HALO = 16
STRIPE = 32
PACKED = 40
PICKS = 40
LONG = 1024
MAXOFF = 98
FAR = 256
f32 = jnp.float32
bf16 = jnp.bfloat16
VM = pl.BlockSpec(memory_space=pltpu.VMEM)
HB = pl.BlockSpec(memory_space=pltpu.HBM)
SM = pl.BlockSpec(memory_space=pltpu.SMEM)
LIMIT = pltpu.CompilerParams(vmem_limit_bytes=32 * 2**20)


def hermite_table():
    t = (np.arange(TAPS, dtype=np.float32) - np.float32(RAD)) / np.float32(4.0)
    series = [np.ones(t.shape, np.float32), np.float32(2.0) * t]
    for n in range(1, ORDERS - 1):
        series.append(np.float32(2.0) * t * series[n] - np.float32(2.0 * n) * series[n - 1])
    w = np.stack(series) * np.exp(np.float32(-0.5) * t * t)
    w = w / np.sqrt(np.sum(w * w, axis=1, keepdims=True))
    return np.asarray(w, dtype=jnp.bfloat16).astype(np.float32)


def quarter(x, k):
    return pltpu.roll(x, (k % 4) * 32, 1) if k % 4 else x


def choose(quarters, *items):
    out = items[-1]
    for mask, item in zip(quarters, items[:-1]):
        out = jnp.where(mask, item, out)
    return out


def quarter_masks(count):
    at = lax.broadcasted_iota(jnp.int32, (count, 128), 1) // 32
    return [at == k for k in range(3)]


def transpose_quarters(items, masks):
    turned = [quarter(x, j) for j, x in enumerate(items)]
    return [
        quarter(choose(masks, *(turned[(m - t) % 4] for m in range(4))), -t) for t in range(4)
    ]


def across_band(taps):
    band = np.zeros((FAR, ORDERS * 128), np.float32)
    for i in range(ORDERS):
        for x in range(128):
            band[x : x + TAPS, i * 128 + x] = taps[i]
    return band


def scatter_rows():
    r = lax.broadcasted_iota(jnp.int32, (256, 256), 0)
    c = lax.broadcasted_iota(jnp.int32, (256, 256), 1)
    return jnp.where(c == (r % 8) * 32 + r // 8, 1.0, 0.0).astype(bf16)


def gather_rows():
    r = lax.broadcasted_iota(jnp.int32, (256, 256), 0)
    c = lax.broadcasted_iota(jnp.int32, (256, 256), 1)
    source = ((r % 16) * 2 + (r // 16) % 2) * 8 + r // 32
    return jnp.where(c == source, 1.0, 0.0).astype(bf16)


def pack_kernel(
    cells_any, owner_any, index_any, oy_any, ox_any, out_ref,
    cells_ref, owner_ref, index_ref, oy_ref, ox_ref, info_ref, sem,
):
    copies = [
        pltpu.make_async_copy(src, dst, sem.at[k])
        for k, (src, dst) in enumerate(
            (
                (cells_any, cells_ref), (owner_any, owner_ref), (index_any, index_ref),
                (oy_any, oy_ref), (ox_any, ox_ref),
            )
        )
    ]
    for copy in copies:
        copy.start()
    move = scatter_rows()
    masks = quarter_masks(256)
    info_ref[...] = jnp.zeros((8, 128), f32)
    for copy in copies[1:]:
        copy.wait()
    info_ref[0:1, 0:36] = owner_ref[...].astype(f32)
    info_ref[1:2, 0:36] = index_ref[...].astype(f32)
    info_ref[2:3, 0:VISITS] = oy_ref[...].astype(f32)
    info_ref[3:4, 0:VISITS] = ox_ref[...].astype(f32)
    info = info_ref[...].astype(bf16)
    for d in range(GROUP):
        out_ref[d // 2, d % 2, STRIPE:PACKED, :] = info
    copies[0].wait()
    moved = []
    for q in range(4):
        halves = [
            cells_ref[h * 8 : (h + 1) * 8, q * 32 : (q + 1) * 32, :].reshape(256, 128)
            for h in range(2)
        ]
        moved.append(
            jnp.dot(move, jnp.concatenate(halves, axis=1), preferred_element_type=f32)
        )
    for h in range(2):
        groups = transpose_quarters([m[:, h * 128 : (h + 1) * 128] for m in moved], masks)
        for c in range(2):
            for u in range(2):
                at = u * CELLS + h * 8
                out_ref[:, c, at : at + 8, :] = groups[c + 2 * u].reshape(32, 8, 128).astype(bf16)


def select_kernel(me_ref, stripes_ref, out_ref, asks_ref):
    table = jnp.concatenate(
        [
            stripes_ref[:, 0:CELLS, :].reshape(GROUP * CELLS, 128),
            stripes_ref[:, CELLS:STRIPE, :].reshape(GROUP * CELLS, 128),
        ],
        axis=1,
    )
    me = me_ref[0]
    own = (me // 2).astype(f32)
    core = (me % 2).astype(f32)
    for n in range(GROUP):
        asks_ref[:, n, :] = stripes_ref[n, STRIPE:PACKED, :].astype(f32)
    ids = asks_ref[0] * CELLS + asks_ref[1]
    tops = asks_ref[2]
    lefts = asks_ref[3]
    lane = lax.broadcasted_iota(jnp.int32, (GROUP, 128), 1)
    number = [(lane + 128 * k).astype(f32) for k in range(GROUP * CELLS // 128)]
    first = (lane // 32 * 32).astype(f32) + own
    masks = quarter_masks(GROUP)
    move = scatter_rows()

    def column(x, k):
        return jnp.broadcast_to(x[:, k : k + 1], (GROUP, 128))

    lines, last = [], []
    fifths = []
    for v in range(VISITS):
        hot = []
        for r in range(6):
            want = column(ids, v * 6 + r)
            hot.append(
                jnp.concatenate(
                    [jnp.where(n == want, 1.0, 0.0).astype(bf16) for n in number], axis=1
                )
            )
        got = jnp.dot(jnp.concatenate(hot, axis=0), table, preferred_element_type=f32)
        above = first >= column(tops, v)
        late = column(lefts, v) >= 32.0 * (core + 1.0)
        whole, fifth = [], []
        for b in range(3):
            for u in range(2):
                upper = got[b * GROUP : (b + 1) * GROUP, u * 128 : (u + 1) * 128]
                lower = got[(3 + b) * GROUP : (4 + b) * GROUP, u * 128 : (u + 1) * 128]
                whole.append(jnp.where(above, upper, quarter(lower, -1)))
                fifth.append(lower)
        whole[0] = jnp.where(late, whole[5], whole[0])
        fifth[0] = jnp.where(late, fifth[5], fifth[0])
        lines += [w.astype(bf16) for w in whole[:5]]
        fifths.append(choose(masks, *(quarter(fifth[k], k) for k in range(4))).astype(bf16))
        last.append(quarter(fifth[4], v))
    lines += fifths
    lines.append(choose(masks, *last[:4]).astype(bf16))
    lines.append(choose(masks, last[4], last[5], last[5], last[5]).astype(bf16))
    lines += [lines[-1], lines[-1]]
    for k in range(PICKS // 8):
        block = jnp.concatenate(
            [
                jnp.concatenate([x[h * 32 : (h + 1) * 32] for x in lines[k * 8 : k * 8 + 8]], axis=0)
                for h in range(2)
            ],
            axis=1,
        )
        moved = jnp.dot(move, block, preferred_element_type=f32)
        for h in range(2):
            out_ref[h * 32 : (h + 1) * 32, k * 8 : k * 8 + 8, :] = (
                moved[:, h * 128 : (h + 1) * 128].reshape(32, 8, 128).astype(bf16)
            )


def bands_kernel(
    oy_ref, coef_ref, taps_ref, psf_ref,
    near_ref, far_ref, colf_ref, rowf_ref, down_ref, toep_ref, shift_ref,
):
    v = pl.program_id(0)

    def spread(row, count):
        return pltpu.roll(jnp.broadcast_to(row, (count, FAR)), 0, 1, stride=1, stride_axis=0)

    @pl.when(v == 0)
    def _():
        for i in range(ORDERS):
            toep_ref[i] = spread(taps_ref[i : i + 1, :], SIDE)

    oy = oy_ref[v]
    for i in range(ORDERS):
        shift_ref[i] = pltpu.roll(toep_ref[i], oy, 1)
    near = lax.broadcasted_iota(jnp.int32, (COLS, COLS), 0) - lax.broadcasted_iota(
        jnp.int32, (COLS, COLS), 1
    )
    colf_ref[0] = jnp.where(
        jnp.abs(near) <= RAD, spread(psf_ref[0, 0:1, :], COLS), 0.0
    ).astype(bf16)
    rowf_ref[0] = spread(psf_ref[0, 1:2, :], SIDE).astype(bf16)

    masks = quarter_masks(16)
    three = lax.broadcasted_iota(jnp.int32, (16, 128), 1) < 96

    def step(g, _):
        row = lax.broadcasted_iota(jnp.int32, (16, 128), 0) + g * 16
        ty = (2.0 * row.astype(f32) + 1.0) / SIDE - 1.0
        bands = [shift_ref[j, pl.ds(g * 16, 16), :] for j in range(ORDERS)]
        first = 0
        fifth = []
        for i in range(ORDERS):
            sums = [None] * 6
            for j in range(ORDERS - i):
                c = [coef_ref[v, (first + j) * 6 + p] for p in range(6)]
                flat = c[0] + ty * (c[2] + ty * c[5])
                slope = c[1] + ty * c[4]
                for part in range(2):
                    band = bands[j][:, part * 128 : (part + 1) * 128]
                    for q, weight in enumerate((flat, slope, c[3])):
                        term = weight * band
                        at = q * 2 + part
                        sums[at] = term if sums[at] is None else sums[at] + term
            first += ORDERS - i
            ends = []
            for q in range(3):
                low, high = sums[q * 2], sums[q * 2 + 1]
                down_ref[pl.ds(q * SIDE + g * 16, 16), i * 128 : (i + 1) * 128] = (
                    low + jnp.where(three, quarter(high, -1), 0.0)
                ).astype(bf16)
                ends.append(quarter(high, i))
            fifth.append(ends)
        for q in range(3):
            row_at = pl.ds(q * SIDE + g * 16, 16)
            down_ref[row_at, 768:896] = choose(masks, *(fifth[i][q] for i in range(4))).astype(
                bf16
            )
            gap = jnp.zeros((16, 128), f32)
            down_ref[row_at, 896:1024] = choose(
                masks, fifth[4][q], fifth[5][q], gap, gap
            ).astype(bf16)
        return 0

    lax.fori_loop(0, SIDE // 16, step, 0)

    @pl.when(v < 3)
    def _():
        near_ref[v] = down_ref[...]

    @pl.when(v >= 3)
    def _():
        far_ref[0] = down_ref[...]


def model_kernel(
    ox_ref, rows_ref, down_ref, across_any, far_any, colf_any, sci_any,
    diff_any, filt_ref, top_ref, bot_ref,
    across_ref, far_ref, colf_ref, sci_ref, diff_ref, win_ref, stack_ref, sem,
):
    whole = [
        pltpu.make_async_copy(src, dst, sem.at[k])
        for k, (src, dst) in enumerate(
            (
                (across_any, across_ref), (colf_any, colf_ref), (sci_any, sci_ref),
                (far_any, far_ref),
            )
        )
    ]
    for copy in whole[:3]:
        copy.start()
    half = GROUP // 2
    move = gather_rows()
    masks = quarter_masks(half)
    lane = lax.broadcasted_iota(jnp.int32, (160, 128), 1)
    lines = []
    for k in range(PICKS // 8):
        block = jnp.concatenate(
            [
                rows_ref[h * 32 : (h + 1) * 32, k * 8 : k * 8 + 8, :].reshape(256, 128)
                for h in range(2)
            ],
            axis=1,
        )
        lines.append(jnp.dot(move, block, preferred_element_type=f32))

    def take(row, c):
        at = (row % 8) * 32 + c * 16
        return jnp.concatenate(
            [lines[row // 8][at : at + 16, h * 128 : (h + 1) * 128] for h in range(2)], axis=0
        )

    def window(v):
        groups = [[take(v * 5 + k, c) for c in range(2)] for k in range(5)]
        blocks = [
            transpose_quarters(
                [groups[k][0], groups[k][1], groups[m][0], groups[m][1]], masks
            )
            for k, m in ((0, 1), (2, 3), (4, 0))
        ]
        e = [take(30 + v, c) for c in range(2)]
        f = [take(36 + v // 4, c) for c in range(2)]
        fifths = [
            choose(masks, e[0], quarter(e[1], 1), quarter(e[0], 1), quarter(e[1], 2)),
            choose(masks, quarter(e[0], 2), quarter(e[1], 3), quarter(e[0], 3), e[1]),
            choose(
                masks, quarter(f[0], -v), quarter(f[1], 1 - v), quarter(e[0], 2), quarter(e[1], 3)
            ),
        ]
        back = 128 - ox_ref[v]
        turned = [
            pltpu.roll(jnp.concatenate(blocks[b] + [fifths[b]], axis=0), back, 1)
            for b in range(3)
        ]
        tiles = [
            jnp.where(lane < back, turned[b], turned[min(b + 1, 2)]).astype(bf16) for b in range(3)
        ]
        for xb in range(2):
            at = v * 320 + xb * 160
            win_ref[at : at + 160, 0:128] = tiles[xb]
            win_ref[at : at + 160, 128:256] = tiles[xb + 1]

    col = lax.broadcasted_iota(jnp.int32, (SIDE, COLS), 1).astype(f32)
    tx = (2.0 * col + 1.0) / COLS - 1.0

    def spread(group):
        at = group[0] * 320
        got = jnp.dot(
            win_ref[at : at + 320 * len(group), :], across_ref[...], preferred_element_type=f32
        ).astype(bf16)
        for n, v in enumerate(group):
            stack_ref[v, 960:LONG, :] = jnp.zeros((LONG - 960, COLS), bf16)
            for xb in range(2):
                row = n * 320 + xb * 160
                for i in range(ORDERS):
                    piece = got[row : row + 160, i * 128 : (i + 1) * 128]
                    low = ORDERS * 128 + i * half
                    cols = slice(xb * 128, (xb + 1) * 128)
                    stack_ref[v, i * 128 : (i + 1) * 128, cols] = piece[0:128]
                    stack_ref[v, low : low + half, cols] = piece[128:160]

    def differ(v):
        down = down_ref[v] if v < 3 else far_ref[v - 3]
        parts = jnp.dot(down, stack_ref[v], preferred_element_type=f32)
        model = parts[0:128] + tx * (parts[128:256] + tx * parts[256:384])
        diff_ref[v] = (sci_ref[v].astype(f32) - model).astype(bf16)

    def columns(v):
        filt = jnp.dot(diff_ref[v], colf_ref[v], preferred_element_type=f32).astype(bf16)
        filt_ref[v] = filt
        top_ref[v] = filt[0:HALO]
        bot_ref[v] = filt[SIDE - HALO :]

    early, rest = (0, 1, 2), (3, 4, 5)
    for v in (0, 1, 2, 3):
        window(v)
    whole[0].wait()
    whole[3].start()
    spread(early)
    for v in (4, 5):
        window(v)
    spread(rest)
    for copy in whole[1:3]:
        copy.wait()
    for v in early:
        differ(v)
    for v in early:
        columns(v)
    whole[3].wait()
    out = [
        pltpu.make_async_copy(diff_ref.at[n : n + 3], diff_any.at[n : n + 3], sem.at[4 + n // 3])
        for n in (0, 3)
    ]
    out[0].start()
    for v in rest:
        differ(v)
    out[1].start()
    for v in rest:
        columns(v)
    for copy in out:
        copy.wait()


def score_kernel(filt_ref, rowf_any, score_any, part_ref, rowf_ref, score_ref, sem):
    rows = pltpu.make_async_copy(rowf_any, rowf_ref, sem.at[0])
    rows.start()
    rows.wait()
    for v in range(VISITS):
        score = jnp.dot(rowf_ref[v, :, 0:128], filt_ref[v], preferred_element_type=f32)
        score_ref[v] = score
        part_ref[v, 0:HALO] = score[0:HALO]
        part_ref[v, HALO:] = score[SIDE - HALO :]
    done = pltpu.make_async_copy(score_ref, score_any, sem.at[1])
    done.start()
    done.wait()


def edge_kernel(part_ref, above_ref, below_ref, rowf_ref, _, score_ref, buf_ref, sem):
    for v in range(VISITS):
        gap = jnp.zeros((128 - 2 * HALO, COLS), bf16)
        ring = jnp.concatenate([below_ref[v], gap, above_ref[v]], axis=0)
        band = jnp.concatenate(
            [rowf_ref[v, 0:HALO, 128:256], rowf_ref[v, SIDE - HALO :, 128:256]], axis=0
        )
        buf_ref[v] = part_ref[v] + jnp.dot(band, ring, preferred_element_type=f32)
    top = pltpu.make_async_copy(buf_ref.at[:, 0:HALO], score_ref.at[:, 0:HALO], sem.at[0])
    bot = pltpu.make_async_copy(
        buf_ref.at[:, HALO : 2 * HALO], score_ref.at[:, SIDE - HALO : SIDE], sem.at[1]
    )
    top.start()
    bot.start()
    top.wait()
    bot.wait()


def sds(shape, dtype):
    return jax.ShapeDtypeStruct(shape, dtype)


def near(x):
    return pltpu.with_memory_space_constraint(x, pltpu.VMEM)


def body(
    science, templates, cell_owner, cell_index, row_offset, col_offset, coefficients, psf_taps
):
    oy = row_offset[:, 0]
    ox = col_offset[:, 0]
    me = lax.axis_index("sky").astype(jnp.int32).reshape(1)

    packed = pl.pallas_call(
        pack_kernel,
        out_shape=pltpu.VMEM((GROUP // 2, 2, PACKED, 128), bf16),
        in_specs=[HB] * 5,
        out_specs=VM,
        scratch_shapes=[
            pltpu.VMEM((CELLS, SIDE, 128), bf16),
            pltpu.VMEM((1, 36), jnp.int32),
            pltpu.VMEM((1, 36), jnp.int32),
            pltpu.VMEM((1, VISITS), jnp.int32),
            pltpu.VMEM((1, VISITS), jnp.int32),
            pltpu.VMEM((8, 128), f32),
            pltpu.SemaphoreType.DMA((5,)),
        ],
        name="pack",
    )(templates, cell_owner.reshape(1, 36), cell_index, oy.reshape(1, 6), ox.reshape(1, 6))
    stripes = lax.all_to_all(packed.reshape(GROUP, PACKED, 128), "sky", 0, 0, tiled=True)

    taps = hermite_table()
    ahead = np.zeros((8, FAR), np.float32)
    ahead[:ORDERS, :TAPS] = taps
    psf = psf_taps.astype(f32)
    zero = jnp.zeros((VISITS, FAR - TAPS), f32)
    colrow = jnp.concatenate([jnp.flip(psf[:, 1], axis=1), zero], axis=1)
    rowrow = jnp.concatenate([psf[:, 0], zero], axis=1)
    psf_rows = jnp.stack([jnp.roll(colrow, -RAD, axis=1), jnp.roll(rowrow, -RAD, axis=1)], axis=1)

    down, far, colf, rowf = pl.pallas_call(
        bands_kernel,
        grid=(VISITS,),
        in_specs=[
            SM, SM,
            pl.BlockSpec((8, FAR), lambda v: (0, 0)),
            pl.BlockSpec((1, 2, FAR), lambda v: (v, 0, 0)),
        ],
        out_specs=[
            VM,
            pl.BlockSpec((1, 384, LONG), lambda v: (jnp.maximum(v - 3, 0), 0, 0)),
            pl.BlockSpec((1, COLS, COLS), lambda v: (v, 0, 0)),
            pl.BlockSpec((1, SIDE, FAR), lambda v: (v, 0, 0)),
        ],
        out_shape=[
            pltpu.VMEM((3, 384, LONG), bf16),
            sds((3, 384, LONG), bf16),
            sds((VISITS, COLS, COLS), bf16),
            sds((VISITS, SIDE, FAR), bf16),
        ],
        scratch_shapes=[
            pltpu.VMEM((384, LONG), bf16),
            pltpu.VMEM((ORDERS, SIDE, FAR), f32),
            pltpu.VMEM((ORDERS, SIDE, FAR), f32),
        ],
        name="bands",
    )(oy, coefficients.reshape(VISITS, 126), jnp.asarray(ahead), psf_rows)
    stripes, colf = lax.optimization_barrier((stripes, colf))

    picked = pl.pallas_call(
        select_kernel,
        out_shape=sds((GROUP, PICKS, 128), bf16),
        in_specs=[SM, VM],
        out_specs=VM,
        scratch_shapes=[pltpu.VMEM((8, GROUP, 128), f32)],
        compiler_params=LIMIT,
        name="select",
    )(me, near(stripes))
    rows = lax.all_to_all(picked, "sky", 0, 0, tiled=True)

    difference, filtered, top, bot = pl.pallas_call(
        model_kernel,
        in_specs=[SM, VM, VM] + [HB] * 4,
        out_specs=[HB, VM, VM, VM],
        out_shape=[
            sds((VISITS, SIDE, COLS), bf16),
            pltpu.VMEM((VISITS, SIDE, COLS), bf16),
            pltpu.VMEM((VISITS, HALO, COLS), bf16),
            pltpu.VMEM((VISITS, HALO, COLS), bf16),
        ],
        scratch_shapes=[
            pltpu.VMEM((FAR, 768), bf16),
            pltpu.VMEM((3, 384, LONG), bf16),
            pltpu.VMEM((VISITS, COLS, COLS), bf16),
            pltpu.VMEM((VISITS, SIDE, COLS), bf16),
            pltpu.VMEM((VISITS, SIDE, COLS), bf16),
            pltpu.VMEM((VISITS * 320, 256), bf16),
            pltpu.VMEM((VISITS, LONG, COLS), bf16),
            pltpu.SemaphoreType.DMA((6,)),
        ],
        name="model",
    )(ox, near(rows), near(down), jnp.asarray(across_band(taps)).astype(bf16), far, colf, science)

    count = lax.axis_size("ccd")
    above = lax.ppermute(bot, "ccd", [(i, i + 1) for i in range(count - 1)])
    below = lax.ppermute(top, "ccd", [(i + 1, i) for i in range(count - 1)])

    score, part = pl.pallas_call(
        score_kernel,
        in_specs=[VM, HB],
        out_specs=[HB, VM],
        out_shape=[
            sds((VISITS, SIDE, COLS), f32),
            pltpu.VMEM((VISITS, 2 * HALO, COLS), f32),
        ],
        scratch_shapes=[
            pltpu.VMEM((VISITS, SIDE, FAR), bf16),
            pltpu.VMEM((VISITS, SIDE, COLS), f32),
            pltpu.SemaphoreType.DMA((2,)),
        ],
        compiler_params=LIMIT,
        name="score",
    )(near(filtered), rowf)

    score = pl.pallas_call(
        edge_kernel,
        out_shape=sds((VISITS, SIDE, COLS), f32),
        in_specs=[VM, VM, VM, VM, pl.BlockSpec(memory_space=pl.ANY)],
        out_specs=pl.BlockSpec(memory_space=pl.ANY),
        scratch_shapes=[pltpu.VMEM((VISITS, 2 * HALO, COLS), f32), pltpu.SemaphoreType.DMA((2,))],
        input_output_aliases={4: 0},
        compiler_params=LIMIT,
        name="edges",
    )(part, near(above), near(below), rowf, score)
    return difference, score


def solution(mesh):
    in_specs = (
        P("sky", "ccd", None),
        P("sky", "ccd", None),
        P("sky", "ccd", None),
        P("sky", "ccd"),
        P("sky", "ccd"),
        P("sky", "ccd"),
        P("sky", "ccd", None, None),
        P("sky", None, None),
    )
    out_specs = (P("sky", "ccd", None), P("sky", "ccd", None))
    return jax.shard_map(body, mesh=mesh, in_specs=in_specs, out_specs=out_specs, check_vma=False)
```
